32 devices in a mesh: kz: 4 (over x, core), en: 2 (over y), sp: 4 (over z).
Axes of the slice: x: 2, y: 2, z: 4, core: 2. Of those that a mesh axis runs over, the one named last changes fastest.
Arguments:
- green: float32 [4, 4, 4, 2, 256, 256], P('kz', 'en', 'sp'), may hold values from -0.1 to 0.1
- coupling: float32 [4, 3, 256, 256], P('sp'), may hold values from -0.375 to 0.375
- phonon_weight: float32 [3], replicated, may hold values from 0.2 to 0.6
- mode_index: int32 [4, 5], P('kz'), may hold values from 0 to 2
- onsite: float32 [4, 256], P('sp'), may hold values from 0.8 to 1.2
- hopping: float32 [4, 256], P('sp'), may hold values from 0.45 to 0.95
- energies: float32 [4], P('en'), may hold values from -0.1 to 0.1
- guess_scale: float32 [4, 4, 4], P('kz', 'en', 'sp'), may hold values from 0.45 to 0.75
Outputs:
- boundary: float32 [4, 4, 4, 2, 256, 256], P('kz', 'en', 'sp')
The draws below stay inside these ranges and needn't reach their ends.
All inputs are finite; a program needn't handle non-finite values.
Results may differ from the reference program's by a relative error of at most 0.0003.
Values sent between devices are 32-bit elements; how exact they have to be, the bound alone decides.
A program may use at most 64 MiB of HBM per device.

```python
import math
import jax
import jax.numpy as jnp
from jax import lax

NB = 256
MODES = 3
REACH = 2
NEWTON = 3
KZ = 4
NE = 4
NSLAB = 4


def plant(values, rng, least, largest):
    spot = [jax.random.randint(jax.random.fold_in(rng, axis), (), 0, length) for axis, length in enumerate(values.shape)]
    main_axis = values.shape.index(max(values.shape))
    next_to = spot[:main_axis] + [(spot[main_axis] + 1) % values.shape[main_axis]] + spot[main_axis + 1:]
    return values.at[tuple(spot)].set(least).at[tuple(next_to)].set(largest)


def steps_of(rng, extent, shards, low, largest):
    def one(axis_at, blocks):
        draws = jax.random.uniform(jax.random.fold_in(jax.random.fold_in(rng, 6), axis_at), (blocks,), jnp.float32, low / len(shards), largest / len(shards))
        return jnp.repeat(jnp.exp(draws), extent[axis_at] // blocks).reshape((-1,) + (1,) * (len(extent) - axis_at - 1))

    gain = one(*shards[0])
    for cut in shards[1:]:
        gain = gain * one(*cut)
    return gain


def bell_draw(own_key, shape, scale, most, shards=(), held_as=jnp.bfloat16):
    gain = steps_of(own_key, shape, shards, -0.22, 0.18) if shards else 1.0
    values = jax.random.normal(own_key, shape, jnp.float32) * scale * gain
    return jnp.minimum(jnp.maximum(values, -most), most).astype(held_as)


def setup_inputs(seed: int = 0) -> dict:
    arg_keys = jax.random.split(jax.random.key(seed), 9)
    return {
        "green": bell_draw(arg_keys[0], (KZ, NE, NSLAB, 2, NB, NB), 0.012, 0.1, ((0, 4), (1, 2), (2, 4)), jnp.float32),
        "coupling": bell_draw(arg_keys[1], (NSLAB, MODES, NB, NB), NB ** -0.5, 0.375, ((0, 4),), jnp.float32),
        "phonon_weight": jnp.clip(jnp.exp(jax.random.uniform(arg_keys[2], (MODES,), jnp.float32, math.log(0.2), math.log(0.6))), 0.2, 0.6),
        "mode_index": plant(jax.random.randint(arg_keys[3], (KZ, 2 * REACH + 1), 0, MODES), jax.random.fold_in(arg_keys[3], 1), 0, MODES - 1).astype(jnp.int32),
        "onsite": jnp.clip(0.8 + 0.40000004 * jax.random.uniform(arg_keys[4], (NSLAB, NB), jnp.float32) ** steps_of(arg_keys[4], (NSLAB, NB), ((0, 4),), -0.2, 0.2), 0.8, 1.2),
        "hopping": jnp.clip(jnp.exp(math.log(0.95) - 0.74721442 * jax.random.uniform(arg_keys[5], (NSLAB, NB), jnp.float32) ** steps_of(arg_keys[5], (NSLAB, NB), ((0, 4),), -0.2, 0.2)), 0.45, 0.95),
        "energies": jnp.clip(jax.random.uniform(arg_keys[6], (NE,), jnp.float32, -0.1, 0.1) * steps_of(arg_keys[6], (NE,), ((0, 2),), -0.4, 0.0), -0.1, 0.1),
        "guess_scale": jnp.clip(0.45 + 0.3 * jax.random.uniform(arg_keys[7], (KZ, NE, NSLAB), jnp.float32) ** steps_of(arg_keys[7], (KZ, NE, NSLAB), ((0, 4), (1, 2), (2, 4)), -0.2, 0.2), 0.45, 0.75),
    }


HIGHEST_PRECISION = lax.Precision.HIGHEST


def sandwich(matrix, blocks):
    left_product = jnp.einsum('ab,nbc->nac', matrix, blocks, precision=HIGHEST_PRECISION)
    return jnp.einsum('nac,dc->nad', left_product, matrix, precision=HIGHEST_PRECISION)


def batched(first, second):
    return jnp.einsum('...ab,...bc->...ac', first, second, precision=HIGHEST_PRECISION)


def reference(green, coupling, phonon_weight, mode_index, onsite, hopping, energies, guess_scale):
    mode_range = jnp.arange(MODES, dtype=jnp.int32)
    identity = jnp.eye(NB, dtype=jnp.float32)

    def slab_step(boundary, inputs):
        green_slab, couplings, onsite_slab, hop_slab, guess_slab = inputs
        scattered = jnp.zeros(green_slab.shape, jnp.float32)
        for column in range(2 * REACH + 1):
            offset = column - REACH
            shifted = jnp.roll(green_slab, offset, axis=0)

            def per_point(pair):
                index_row, blocks = pair
                selector = (index_row[column] == mode_range).astype(jnp.float32)
                matrix = jnp.sum(selector[:, None, None] * couplings, axis=0)
                weight = jnp.sum(selector * phonon_weight)
                flat = blocks.reshape(-1, NB, NB)
                return (weight * sandwich(matrix, flat)).reshape(blocks.shape)

            scattered = scattered + lax.map(per_point, (mode_index, shifted))
        padded = jnp.pad(scattered, ((0, 0), (1, 1), (0, 0), (0, 0), (0, 0)))
        self_energy = padded[:, :-2] + padded[:, 2:]
        diagonal_shift = onsite_slab[None, :] - energies[:, None]
        system_re = self_energy[:, :, 0] + identity * diagonal_shift[None, :, None, :]
        system_im = self_energy[:, :, 1]
        guess = guess_slab[:, :, None, None]
        inverse_re = 2.0 * guess * identity - guess * guess * system_re
        inverse_im = -(guess * guess) * system_im
        for step in range(NEWTON - 1):
            product_re = batched(system_re, inverse_re) - batched(system_im, inverse_im)
            product_im = batched(system_re, inverse_im) + batched(system_im, inverse_re)
            residual_re = 2.0 * identity - product_re
            residual_im = -product_im
            inverse_re, inverse_im = (batched(inverse_re, residual_re) - batched(inverse_im, residual_im),
                                      batched(inverse_re, residual_im) + batched(inverse_im, residual_re))
        inverse = jnp.stack([inverse_re, inverse_im], axis=2)
        outer_hop = hop_slab[:, None] * hop_slab[None, :]
        boundary = outer_hop * boundary + inverse
        return boundary, boundary

    start = jnp.zeros((KZ, NE, 2, NB, NB), jnp.float32)
    inputs = (jnp.moveaxis(green, 2, 0), coupling, onsite, hopping, jnp.moveaxis(guess_scale, 2, 0))
    final_state, stacked = lax.scan(slab_step, start, inputs)
    return jnp.moveaxis(stacked, 0, 2)
```

```python
import functools

import jax
import jax.numpy as jnp
from jax import lax
from jax.experimental import pallas as pl
from jax.experimental.pallas import tpu as pltpu
from jax.sharding import PartitionSpec as P

REACH = 2
ROW_BLOCKS = 8
MESH = pl.DeviceIdType.MESH


def split(value):
    high = value.astype(jnp.bfloat16)
    return high, (value - high.astype(jnp.float32)).astype(jnp.bfloat16)


def dot_split(first, second):
    left = jnp.concatenate([first[0], first[0], first[1]], axis=1)
    right = jnp.concatenate([second[0], second[1], second[0]], axis=0)
    return jnp.dot(left, right, preferred_element_type=jnp.float32)


def complex_pair(re, im):
    return jnp.concatenate(
        [jnp.concatenate([re, -im], axis=1), jnp.concatenate([im, re], axis=1)], axis=0
    )


def kernel(
    sizes,
    mode_in, weight_in, energy_in, guess_in, green_in, coupling_in, onsite_in, hopping_in,
    out_ref,
    mode_ref, mode_sib, mode_far, weight_ref, energy_ref, guess_ref,
    green_ref, coupling_ref, onsite_ref, hopping_ref,
    halo, left3, right3, block3, terms, total, sib_out, sib_in, part_out, part_in, message, arrived,
    inverse, before, outer,
    small_sem, coupling_sem, green_sem, mode_send, mode_recv, halo_send, halo_recv,
    sib_send, sib_recv, part_send, part_recv, kz_send, kz_recv, sp_send, sp_recv,
):
    kz_count, en_count, sp_count = sizes
    energy_count, _, n, _ = green_ref.shape
    modes = coupling_ref.shape[0]
    ring = kz_count > 2 * REACH
    steps = (REACH, -REACH) if ring else (REACH,)
    messages = [(d, t) for d in range(len(steps)) for t in range(2)]
    half = n // 2
    rows = n // ROW_BLOCKS
    pieces = 2 * ROW_BLOCKS
    k, en, sp = lax.axis_index("kz"), lax.axis_index("en"), lax.axis_index("sp")
    odd = lax.rem(k, 2)
    base = k - odd
    sibling = base + 1 - odd

    def far(d, t):
        return lax.rem(base + t + steps[d] + kz_count, kz_count)

    def origin(d, t):
        return lax.rem(base + t - steps[d] + kz_count, kz_count)

    def green_load(e, p):
        return pltpu.make_async_copy(green_in.at[e, p], green_ref.at[e, p], green_sem.at[e, p])

    coupling_load = pltpu.make_async_copy(coupling_in, coupling_ref, coupling_sem)
    small_loads = [
        pltpu.make_async_copy(source, target, small_sem.at[index])
        for index, (source, target) in enumerate((
            (mode_in, mode_ref), (weight_in, weight_ref), (energy_in, energy_ref),
            (guess_in, guess_ref), (onsite_in, onsite_ref), (hopping_in, hopping_ref),
        ))
    ]
    coupling_load.start()
    for p in range(2):
        for e in range(energy_count):
            green_load(e, p).start()
    for load in small_loads:
        load.start()

    barrier = pltpu.get_barrier_semaphore()

    def greet(axis, index):
        pl.semaphore_signal(barrier, inc=1, device_id={axis: index}, device_id_type=MESH)

    greet("kz", sibling)
    for d, t in messages:
        greet("kz", far(d, t))
    for axis, here, count in (("en", en, en_count), ("sp", sp, sp_count)):
        pl.when(here > 0)(lambda axis=axis, here=here: greet(axis, here - 1))
        pl.when(here < count - 1)(lambda axis=axis, here=here: greet(axis, here + 1))
    expected = 1 + len(messages)
    for here, count in ((en, en_count), (sp, sp_count)):
        expected = expected + (here > 0).astype(jnp.int32) + (here < count - 1).astype(jnp.int32)
    pl.semaphore_wait(barrier, expected)

    def remote(source, target, send, recv, axis, index):
        return pltpu.make_async_remote_copy(
            src_ref=source, dst_ref=target, send_sem=send, recv_sem=recv,
            device_id={axis: index}, device_id_type=MESH,
        )

    def halo_up(p):
        return remote(green_in.at[energy_count - 1, p], halo.at[0, p],
                      halo_send.at[0, p], halo_recv.at[0, p], "en", en + 1)

    def halo_down(p):
        return remote(green_in.at[0, p], halo.at[1, p],
                      halo_send.at[1, p], halo_recv.at[1, p], "en", en - 1)

    def mode_to_sibling():
        return remote(mode_in, mode_sib, mode_send.at[2 * len(steps) * 2],
                      mode_recv.at[len(messages)], "kz", sibling)

    def mode_to_origin(d, t, slot):
        return remote(mode_in, mode_far.at[2 * d + slot], mode_send.at[2 * d + t],
                      mode_recv.at[2 * d + slot], "kz", origin(d, t))

    mode_to_sibling().start()
    for d, t in messages:
        mode_to_origin(d, t, odd).start()
    for p in range(2):
        pl.when(en < en_count - 1)(lambda p=p: halo_up(p).start())
        pl.when(en > 0)(lambda p=p: halo_down(p).start())

    @pl.when(en == 0)
    def _():
        halo[0] = jnp.zeros_like(halo[0])

    @pl.when(en == en_count - 1)
    def _():
        halo[1] = jnp.zeros_like(halo[1])

    def energy_of(i):
        return lax.rem(i + en, energy_count)

    def load_block(i, p):
        e = energy_of(i)

        def keep(value):
            high, low = split(value)
            block3[0:n] = high
            block3[n:2 * n] = low
            block3[2 * n:] = high

        below = green_ref[jnp.maximum(e - 1, 0), p]
        above = green_ref[jnp.minimum(e + 1, energy_count - 1), p]

        @pl.when((e > 0) & (e < energy_count - 1))
        def _():
            keep(below + above)

        @pl.when(e == 0)
        def _():
            pl.when(en > 0)(lambda: halo_up(p).wait_recv())
            keep(halo[0, p] + above)

        @pl.when((e > 0) & (e == energy_count - 1))
        def _():
            pl.when(en < en_count - 1)(lambda: halo_down(p).wait_recv())
            keep(below + halo[1, p])

    def mode_terms(side):
        first = jnp.dot(left3[side], block3[...], preferred_element_type=jnp.float32)
        for m in range(modes):
            high, low = split(first[m * half:(m + 1) * half])
            terms[m] = jnp.dot(
                jnp.concatenate([high, high, low], axis=1), right3[m],
                preferred_element_type=jnp.float32,
            )

    def contribution(d, t):
        row = mode_far.at[2 * d + t]
        same = odd == t
        near = 2 * REACH - 1 if t == 0 else 1
        if not ring:
            mode = jnp.where(same, row[2 * REACH], row[near])
            other = row[0]
            return terms[mode] + same.astype(jnp.float32) * terms[other]
        end = 2 * REACH if d == 0 else 0
        if t == d:
            return terms[jnp.where(same, row[end], row[near])]
        return same.astype(jnp.float32) * terms[row[end]]

    def to_sibling(i, p):
        return remote(sib_out.at[i, p], sib_in.at[i, p], sib_send.at[i, p],
                      sib_recv.at[i, p], "kz", sibling)

    def part(i, p, j):
        return remote(part_out.at[i, p, j], part_in.at[i, p, j], part_send.at[i, p, j],
                      part_recv.at[i, p, j], "kz", sibling)

    def over(i, p, j, side):
        d, t = messages[j]
        return remote(message.at[i, p, j],
                      arrived.at[d, i, p, pl.ds(pl.multiple_of(side * half, half), half)],
                      kz_send.at[i, p, j], kz_recv.at[d, i, p, side], "kz", far(d, t))

    def half_terms(i, p, own):
        side = odd if own else 1 - odd
        mode_terms(side)
        at = pl.ds(pl.multiple_of(side * half, half), half)
        for j, (d, t) in enumerate(messages):
            if own:
                message[i, p, j] = contribution(d, t)
            else:
                part_out[i, p, j] = contribution(d, t)
                part(i, p, j).start()
        sib_out[i, p, at] = terms[mode_sib[REACH + 1 - 2 * odd]]
        if own:
            to_sibling(i, p).start()
        total[i, p, at] = terms[mode_ref[REACH]]

    def assemble(i, p, j):
        part(i, p, j).wait_recv()
        message[i, p, j] += part_in[i, p, j]
        over(i, p, j, odd).start()

    def gather(i, p):
        to_sibling(i, p).wait_recv()
        total[i, p] += sib_in[i, p]

    def collect(i, p):
        value = total[i, p]
        for d in range(len(steps)):
            for side in range(2):
                over(i, p, 2 * d, side).wait_recv()
            value = value + arrived[d, i, p]
        return value

    def place(j):
        block, rest = j // ROW_BLOCKS, lax.rem(j, ROW_BLOCKS)
        p, r = rest // (ROW_BLOCKS // 2), lax.rem(rest, ROW_BLOCKS // 2)
        return p, pl.ds(pl.multiple_of(block * half + r * rows, rows), rows)

    def link(i, j):
        p, at = place(j)
        return remote(out_ref.at[energy_of(i), p, at], before.at[i, p, at],
                      sp_send.at[i, j], sp_recv.at[i, j], "sp", sp + 1)

    def chain_step(i, j):
        p, at = place(j)
        e = energy_of(i)

        @pl.when(sp > 0)
        def _():
            link(i, j).wait_recv()
            out_ref[e, p, at] = outer[at] * before[i, p, at] + inverse[i, p, at]

        @pl.when(sp == 0)
        def _():
            out_ref[e, p, at] = inverse[i, p, at]

        @pl.when(sp < sp_count - 1)
        def _():
            link(i, j).start()

    def chain_part(i, first, last):
        @pl.loop(first, last)
        def _(j):
            chain_step(i, j)

    def invert(i):
        e = energy_of(i)
        guess = guess_ref[e]
        shift = onsite_ref[...] - energy_ref[e]
        diagonal = (lax.broadcasted_iota(jnp.int32, (n, n), 0)
                    == lax.broadcasted_iota(jnp.int32, (n, n), 1))
        r_re = jnp.where(diagonal, 1.0 - guess * shift, 0.0) - guess * collect(i, 0)
        r_im = -guess * collect(i, 1)

        def stack(re, im):
            return tuple(
                jnp.concatenate([a, b], axis=0) for a, b in zip(split(re), split(im))
            )

        def left(re, im):
            return tuple(complex_pair(a, b) for a, b in zip(split(re), split(im)))

        r_left = left(r_re, r_im)
        square = dot_split(r_left, stack(r_re, r_im))
        s_re, s_im = square[:n], square[n:]
        s_stack = stack(s_re, s_im)
        cube = dot_split(r_left, s_stack)
        fourth = dot_split(left(s_re, s_im), s_stack)
        one = jnp.where(diagonal, 1.0, 0.0)
        p_re = one + r_re + s_re + cube[:n]
        p_im = r_im + s_im + cube[n:]
        re, im = split(p_re), split(p_im)
        fourth = stack(fourth[:n], fourth[n:])
        for block in range(2):
            at = slice(block * half, (block + 1) * half)
            rows_left = tuple(complex_pair(a[at], b[at]) for a, b in zip(re, im))
            result = dot_split(rows_left, fourth)
            inverse[i, 0, at] = guess * (p_re[at] + result[:half])
            inverse[i, 1, at] = guess * (p_im[at] + result[half:])
            pl.when(sp == 0)(lambda: chain_part(i, block * ROW_BLOCKS, (block + 1) * ROW_BLOCKS))

    for load in small_loads:
        load.wait()
    coupling_load.wait()
    for mode in range(modes):
        matrix = coupling_ref[mode]
        high, low = split(matrix)
        for side in range(2):
            at = slice(mode * half, (mode + 1) * half)
            here = slice(side * half, (side + 1) * half)
            left3[side, at] = jnp.concatenate([high[here], high[here], low[here]], axis=1)
        high, low = split(matrix.T * weight_ref[mode])
        right3[mode] = jnp.concatenate([high, low, high], axis=0)
    for p in range(2):
        for e in range(energy_count):
            green_load(e, p).wait()

    evens = [j for j, (d, t) in enumerate(messages) if t == 0]
    odds = [j for j, (d, t) in enumerate(messages) if t == 1]

    def wait_modes():
        mode_to_sibling().wait_recv()
        for d, t in messages:
            mode_to_origin(d, t, t).wait_recv()

    load_block(0, 0)
    wait_modes()
    half_terms(0, 0, False)
    half_terms(0, 0, True)
    load_block(0, 1)
    half_terms(0, 1, False)
    for j in evens:
        assemble(0, 0, j)
    half_terms(0, 1, True)
    for j in evens:
        assemble(0, 1, j)
    for j in odds:
        for p in range(2):
            assemble(0, p, j)
    across = jnp.broadcast_to(hopping_ref[...], (n, n))
    outer[...] = across * across.T
    for i in range(energy_count):
        last = i == energy_count - 1

        def second(i=i):
            load_block(i + 1, 1)
            half_terms(i + 1, 1, False)
            half_terms(i + 1, 1, True)
            for j in evens:
                assemble(i + 1, 1, j)
            for j in odds:
                for p in range(2):
                    assemble(i + 1, p, j)

        for p in range(2):
            gather(i, p)
        if not last:
            load_block(i + 1, 0)
            half_terms(i + 1, 0, False)
            half_terms(i + 1, 0, True)
            for j in evens:
                assemble(i + 1, 0, j)
            pl.when(odd == 1)(second)
        invert(i)
        if not last:
            pl.when(odd == 0)(second)
        pl.when(sp > 0)(lambda i=i: chain_part(i, 0, pieces))

    mode_to_sibling().wait_send()
    for d, t in messages:
        mode_to_origin(d, t, odd).wait_send()
    for p in range(2):
        pl.when(en < en_count - 1)(lambda p=p: halo_up(p).wait_send())
        pl.when(en > 0)(lambda p=p: halo_down(p).wait_send())
    for i in range(energy_count):
        for p in range(2):
            to_sibling(i, p).wait_send()
            for j in range(len(messages)):
                part(i, p, j).wait_send()
                over(i, p, j, odd).wait_send()

        @pl.when(sp < sp_count - 1)
        def _():
            @pl.loop(0, pieces)
            def _(j):
                link(i, j).wait_send()


def body(sizes, green, coupling, phonon_weight, mode_index, onsite, hopping, energies, guess_scale):
    energy_count, n = green.shape[1], green.shape[-1]
    modes = coupling.shape[1]
    blocks = (energy_count, 2, n, n)
    steps = 2 if sizes[0] > 2 * REACH else 1
    halves = (energy_count, 2, 2 * steps, n // 2, n)
    pieces = 2 * ROW_BLOCKS
    hbm = pl.BlockSpec(memory_space=pltpu.HBM)
    vmem = pl.BlockSpec(memory_space=pltpu.VMEM)
    columns = mode_index.shape[1]
    dma = pltpu.SemaphoreType.DMA
    out = pl.pallas_call(
        functools.partial(kernel, sizes),
        out_shape=jax.ShapeDtypeStruct(blocks, jnp.float32),
        in_specs=[hbm] * 8,
        out_specs=vmem,
        scratch_shapes=[
            pltpu.SMEM((columns,), jnp.int32),
            pltpu.SMEM((columns,), jnp.int32),
            pltpu.SMEM((2 * steps, columns), jnp.int32),
            pltpu.SMEM(phonon_weight.shape, jnp.float32),
            pltpu.SMEM((energy_count,), jnp.float32),
            pltpu.SMEM((energy_count,), jnp.float32),
            pltpu.VMEM(blocks, jnp.float32),
            pltpu.VMEM(coupling.shape[1:], jnp.float32),
            pltpu.VMEM((1, n), jnp.float32),
            pltpu.VMEM((1, n), jnp.float32),
            pltpu.VMEM((2, 2, n, n), jnp.float32),
            pltpu.VMEM((2, modes * n // 2, 3 * n), jnp.bfloat16),
            pltpu.VMEM((modes, 3 * n, n), jnp.bfloat16),
            pltpu.VMEM((3 * n, n), jnp.bfloat16),
            pltpu.VMEM((modes, n // 2, n), jnp.float32),
            pltpu.VMEM(blocks, jnp.float32),
            pltpu.VMEM(blocks, jnp.float32),
            pltpu.VMEM(blocks, jnp.float32),
            pltpu.VMEM(halves, jnp.float32),
            pltpu.VMEM(halves, jnp.float32),
            pltpu.VMEM(halves, jnp.float32),
            pltpu.VMEM((steps,) + blocks, jnp.float32),
            pltpu.VMEM(blocks, jnp.float32),
            pltpu.VMEM(blocks, jnp.float32),
            pltpu.VMEM((n, n), jnp.float32),
            dma((6,)),
            dma,
            dma((energy_count, 2)),
            dma((4 * steps + 1,)),
            dma((2 * steps + 1,)),
            dma((2, 2)),
            dma((2, 2)),
            dma((energy_count, 2)),
            dma((energy_count, 2)),
            dma((energy_count, 2, 2 * steps)),
            dma((energy_count, 2, 2 * steps)),
            dma((energy_count, 2, 2 * steps)),
            dma((steps, energy_count, 2, 2)),
            dma((energy_count, pieces)),
            dma((energy_count, pieces)),
        ],
        compiler_params=pltpu.CompilerParams(
            collective_id=0, has_side_effects=True, vmem_limit_bytes=50 << 20
        ),
    )(
        *(
            pltpu.with_memory_space_constraint(value, pltpu.HBM)
            for value in (
                mode_index[0], phonon_weight, energies, guess_scale.reshape(energy_count),
                green.reshape(blocks), coupling[0], onsite, hopping,
            )
        )
    )
    return out.reshape(1, energy_count, 1, 2, n, n)


def solution(mesh):
    placed = (
        P("kz", "en", "sp", None, None, None),
        P("sp", None, None, None),
        P(),
        P("kz", None),
        P("sp", None),
        P("sp", None),
        P("en"),
        P("kz", "en", "sp"),
    )
    sizes = tuple(mesh.shape[axis] for axis in ("kz", "en", "sp"))
    return jax.shard_map(
        functools.partial(body, sizes),
        mesh=mesh,
        in_specs=placed,
        out_specs=P("kz", "en", "sp", None, None, None),
        check_vma=False,
    )
```

```python
import functools

import jax
import jax.numpy as jnp
from jax import lax
from jax.experimental import pallas as pl
from jax.experimental.pallas import tpu as pltpu
from jax.sharding import PartitionSpec as P

REACH = 2
ROW_BLOCKS = 8
MESH = pl.DeviceIdType.MESH


def split(value):
    high = value.astype(jnp.bfloat16)
    return high, (value - high.astype(jnp.float32)).astype(jnp.bfloat16)


def dot_split(first, second):
    left = jnp.concatenate([first[0], first[0], first[1]], axis=1)
    right = jnp.concatenate([second[0], second[1], second[0]], axis=0)
    return jnp.dot(left, right, preferred_element_type=jnp.float32)


def complex_pair(re, im):
    return jnp.concatenate(
        [jnp.concatenate([re, -im], axis=1), jnp.concatenate([im, re], axis=1)], axis=0
    )


def kernel(
    sizes,
    mode_in, weight_in, energy_in, guess_in, green_in, coupling_in, onsite_in, hopping_in,
    out_ref,
    mode_near, mode_far, weight_ref, energy_ref, guess_ref,
    green_ref, coupling_ref, onsite_ref, hopping_ref,
    halo, left3, right3, terms, blocks, near, message, arrived, inverse, before, outer,
    small_sem, coupling_sem, green_sem, mode_send, mode_recv, halo_send, halo_recv,
    block_send, block_recv, near_send, near_recv, kz_send, kz_recv, sp_send, sp_recv,
):
    kz_count, en_count, sp_count = sizes
    energy_count, _, n, _ = green_ref.shape
    modes = coupling_ref.shape[0]
    ring = kz_count > 2 * REACH
    steps = (REACH, -REACH) if ring else (REACH,)
    messages = [(d, t) for d in range(len(steps)) for t in range(2)]
    half = n // 2
    rows = n // ROW_BLOCKS
    pieces = 2 * ROW_BLOCKS
    k, en, sp = lax.axis_index("kz"), lax.axis_index("en"), lax.axis_index("sp")
    odd = lax.rem(k, 2)
    base = k - odd
    sibling = base + 1 - odd

    def far(d, t):
        return lax.rem(base + t + steps[d] + kz_count, kz_count)

    def origin(d, t):
        return lax.rem(base + t - steps[d] + kz_count, kz_count)

    def green_load(e, p):
        return pltpu.make_async_copy(green_in.at[e, p], green_ref.at[e, p], green_sem.at[e, p])

    coupling_load = pltpu.make_async_copy(coupling_in, coupling_ref, coupling_sem)
    small_loads = [
        pltpu.make_async_copy(source, target, small_sem.at[index])
        for index, (source, target) in enumerate((
            (mode_in, mode_near.at[odd]), (weight_in, weight_ref), (energy_in, energy_ref),
            (guess_in, guess_ref), (onsite_in, onsite_ref), (hopping_in, hopping_ref),
        ))
    ]
    for p in range(2):
        for e in range(energy_count):
            green_load(e, p).start()
        if p == 0:
            coupling_load.start()
    for load in small_loads:
        load.start()

    barrier = pltpu.get_barrier_semaphore()

    def greet(axis, index):
        pl.semaphore_signal(barrier, inc=1, device_id={axis: index}, device_id_type=MESH)

    greet("kz", sibling)
    for d, t in messages:
        greet("kz", far(d, t))
    for axis, here, count in (("en", en, en_count), ("sp", sp, sp_count)):
        pl.when(here > 0)(lambda axis=axis, here=here: greet(axis, here - 1))
        pl.when(here < count - 1)(lambda axis=axis, here=here: greet(axis, here + 1))
    expected = 1 + len(messages)
    for here, count in ((en, en_count), (sp, sp_count)):
        expected = expected + (here > 0).astype(jnp.int32) + (here < count - 1).astype(jnp.int32)
    pl.semaphore_wait(barrier, expected)

    def remote(source, target, send, recv, axis, index):
        return pltpu.make_async_remote_copy(
            src_ref=source, dst_ref=target, send_sem=send, recv_sem=recv,
            device_id={axis: index}, device_id_type=MESH,
        )

    def halo_up(p):
        return remote(green_in.at[energy_count - 1, p], halo.at[0, p],
                      halo_send.at[0, p], halo_recv.at[0, p], "en", en + 1)

    def halo_down(p):
        return remote(green_in.at[0, p], halo.at[1, p],
                      halo_send.at[1, p], halo_recv.at[1, p], "en", en - 1)

    def mode_to_sibling(parity):
        return remote(mode_in, mode_near.at[parity], mode_send.at[2 * len(steps)],
                      mode_recv.at[len(messages)], "kz", sibling)

    def mode_to_origin(d, t, slot):
        return remote(mode_in, mode_far.at[2 * d + slot], mode_send.at[2 * d + t],
                      mode_recv.at[2 * d + slot], "kz", origin(d, t))

    mode_to_sibling(odd).start()
    for d, t in messages:
        mode_to_origin(d, t, odd).start()
    for p in range(2):
        pl.when(en < en_count - 1)(lambda p=p: halo_up(p).start())
        pl.when(en > 0)(lambda p=p: halo_down(p).start())

    @pl.when(en == 0)
    def _():
        halo[0] = jnp.zeros_like(halo[0])

    @pl.when(en == en_count - 1)
    def _():
        halo[1] = jnp.zeros_like(halo[1])

    def energy_of(i):
        return lax.rem(i + en, energy_count)

    def swap(i, p, parity):
        return remote(blocks.at[parity, i, p], blocks.at[parity, i, p], block_send.at[i, p],
                      block_recv.at[i, p], "kz", sibling)

    def load_block(i, p):
        e = energy_of(i)
        below = green_ref[jnp.maximum(e - 1, 0), p]
        above = green_ref[jnp.minimum(e + 1, energy_count - 1), p]

        @pl.when((e > 0) & (e < energy_count - 1))
        def _():
            blocks[odd, i, p] = below + above

        @pl.when(e == 0)
        def _():
            pl.when(en > 0)(lambda: halo_up(p).wait_recv())
            blocks[odd, i, p] = halo[0, p] + above

        @pl.when((e > 0) & (e == energy_count - 1))
        def _():
            pl.when(en < en_count - 1)(lambda: halo_down(p).wait_recv())
            blocks[odd, i, p] = below + halo[1, p]

        swap(i, p, odd).start()

    def columns(d, t, source):
        if source == t:
            if not ring:
                return (2 * REACH, 0)
            return (2 * REACH,) if d == 0 else (0,)
        if not ring or t == d:
            return (2 * REACH - 1,) if t == 0 else (1,)
        return ()

    def picked(row, column, source):
        return terms[row[column], pl.ds(source * half, half)]

    def over(i, p, j, side):
        d, t = messages[j]
        return remote(message.at[i, p, j],
                      arrived.at[d, i, p, pl.ds(pl.multiple_of(side * half, half), half)],
                      kz_send.at[i, p, j], kz_recv.at[d, i, p, side], "kz", far(d, t))

    def near_half(i, p, parity, side):
        at = near.at[parity, i, p, pl.ds(pl.multiple_of(side * half, half), half)]
        return remote(at, at, near_send.at[i, p], near_recv.at[i, p], "kz", sibling)

    def block_terms(i, p):
        swap(i, p, 1 - odd).wait_recv()
        first = [
            dot_split((left3[:, :n], left3[:, 2 * n:]), split(blocks[source, i, p]))
            for source in range(2)
        ]
        for m in range(modes):
            at = slice(m * half, (m + 1) * half)
            high, low = split(jnp.concatenate([first[0][at], first[1][at]], axis=0))
            terms[m] = jnp.dot(
                jnp.concatenate([high, high, low], axis=1), right3[m],
                preferred_element_type=jnp.float32,
            )

    def block_messages(i, p):
        for j, (d, t) in enumerate(messages):
            message[i, p, j] = sum(
                picked(mode_far.at[2 * d + t], column, source)
                for source in range(2) for column in columns(d, t, source)
            )
            if t == 0:
                over(i, p, j, odd).start()
        at = pl.ds(pl.multiple_of(odd * half, half), half)
        for t in range(2):
            near[t, i, p, at] = (
                picked(mode_near.at[t], REACH, t)
                + picked(mode_near.at[t], REACH + 2 * t - 1, 1 - t)
            )
        near_half(i, p, 1 - odd, odd).start()

    def send_odds(i):
        for p in range(2):
            for j, (d, t) in enumerate(messages):
                if t == 1:
                    over(i, p, j, odd).start()

    def collect(i, p):
        near_half(i, p, odd, 1 - odd).wait_recv()
        value = near[odd, i, p]
        for d in range(len(steps)):
            for side in range(2):
                over(i, p, 2 * d, side).wait_recv()
            value = value + arrived[d, i, p]
        return value

    def place(j):
        block, rest = j // ROW_BLOCKS, lax.rem(j, ROW_BLOCKS)
        p, r = rest // (ROW_BLOCKS // 2), lax.rem(rest, ROW_BLOCKS // 2)
        return p, pl.ds(pl.multiple_of(block * half + r * rows, rows), rows)

    def link(i, j):
        p, at = place(j)
        return remote(out_ref.at[energy_of(i), p, at], before.at[i, p, at],
                      sp_send.at[i, j], sp_recv.at[i, j], "sp", sp + 1)

    def chain_step(i, j):
        p, at = place(j)
        e = energy_of(i)

        @pl.when(sp > 0)
        def _():
            link(i, j).wait_recv()
            out_ref[e, p, at] = outer[at] * before[i, p, at] + inverse[i, p, at]

        @pl.when(sp == 0)
        def _():
            out_ref[e, p, at] = inverse[i, p, at]

        @pl.when(sp < sp_count - 1)
        def _():
            link(i, j).start()

    def chain_part(i, first, last):
        @pl.loop(first, last)
        def _(j):
            chain_step(i, j)

    def invert(i):
        e = energy_of(i)
        guess = guess_ref[e]
        shift = onsite_ref[...] - energy_ref[e]
        diagonal = (lax.broadcasted_iota(jnp.int32, (n, n), 0)
                    == lax.broadcasted_iota(jnp.int32, (n, n), 1))
        r_re = jnp.where(diagonal, 1.0 - guess * shift, 0.0) - guess * collect(i, 0)
        r_im = -guess * collect(i, 1)

        def stack(re, im):
            return tuple(
                jnp.concatenate([a, b], axis=0) for a, b in zip(split(re), split(im))
            )

        def left(re, im):
            return tuple(complex_pair(a, b) for a, b in zip(split(re), split(im)))

        r_left = left(r_re, r_im)
        square = dot_split(r_left, stack(r_re, r_im))
        s_re, s_im = square[:n], square[n:]
        s_stack = stack(s_re, s_im)
        cube = dot_split(r_left, s_stack)
        fourth = dot_split(left(s_re, s_im), s_stack)
        one = jnp.where(diagonal, 1.0, 0.0)
        p_re = one + r_re + s_re + cube[:n]
        p_im = r_im + s_im + cube[n:]
        re, im = split(p_re), split(p_im)
        fourth = stack(fourth[:n], fourth[n:])
        for block in range(2):
            at = slice(block * half, (block + 1) * half)
            rows_left = tuple(complex_pair(a[at], b[at]) for a, b in zip(re, im))
            result = dot_split(rows_left, fourth)
            inverse[i, 0, at] = guess * (p_re[at] + result[:half])
            inverse[i, 1, at] = guess * (p_im[at] + result[half:])
            pl.when(sp == 0)(lambda: chain_part(i, block * ROW_BLOCKS, (block + 1) * ROW_BLOCKS))

    for e in range(energy_count):
        green_load(e, 0).wait()
    load_block(0, 0)
    for e in range(energy_count):
        green_load(e, 1).wait()
    load_block(0, 1)
    for load in small_loads:
        load.wait()
    coupling_load.wait()
    for m in range(modes):
        at = slice(m * half, (m + 1) * half)
        here = pl.ds(pl.multiple_of(odd * half, half), half)
        high, low = split(coupling_ref[m, here])
        left3[at] = jnp.concatenate([high, high, low], axis=1)
        high, low = split(coupling_ref[m].T * weight_ref[m])
        right3[m] = jnp.concatenate([high, low, high], axis=0)
    block_terms(0, 0)
    mode_to_sibling(1 - odd).wait_recv()
    for d, t in messages:
        mode_to_origin(d, t, t).wait_recv()
    block_messages(0, 0)
    block_terms(0, 1)
    block_messages(0, 1)
    send_odds(0)
    across = jnp.broadcast_to(hopping_ref[...], (n, n))
    outer[...] = across * across.T
    for i in range(energy_count):
        last = i == energy_count - 1

        def second(i=i):
            load_block(i + 1, 1)
            block_terms(i + 1, 1)
            block_messages(i + 1, 1)
            send_odds(i + 1)

        if not last:
            load_block(i + 1, 0)
            block_terms(i + 1, 0)
            block_messages(i + 1, 0)
            pl.when(odd == 1)(second)
        invert(i)
        if not last:
            pl.when(odd == 0)(second)
        pl.when(sp > 0)(lambda i=i: chain_part(i, 0, pieces))

    mode_to_sibling(odd).wait_send()
    for d, t in messages:
        mode_to_origin(d, t, odd).wait_send()
    for p in range(2):
        pl.when(en < en_count - 1)(lambda p=p: halo_up(p).wait_send())
        pl.when(en > 0)(lambda p=p: halo_down(p).wait_send())
    for i in range(energy_count):
        for p in range(2):
            swap(i, p, odd).wait_send()
            near_half(i, p, 1 - odd, odd).wait_send()
            for j in range(len(messages)):
                over(i, p, j, odd).wait_send()

        @pl.when(sp < sp_count - 1)
        def _():
            @pl.loop(0, pieces)
            def _(j):
                link(i, j).wait_send()


def body(sizes, green, coupling, phonon_weight, mode_index, onsite, hopping, energies, guess_scale):
    energy_count, n = green.shape[1], green.shape[-1]
    modes = coupling.shape[1]
    blocks = (energy_count, 2, n, n)
    steps = 2 if sizes[0] > 2 * REACH else 1
    halves = (energy_count, 2, 2 * steps, n // 2, n)
    pieces = 2 * ROW_BLOCKS
    hbm = pl.BlockSpec(memory_space=pltpu.HBM)
    vmem = pl.BlockSpec(memory_space=pltpu.VMEM)
    columns = mode_index.shape[1]
    dma = pltpu.SemaphoreType.DMA
    out = pl.pallas_call(
        functools.partial(kernel, sizes),
        out_shape=jax.ShapeDtypeStruct(blocks, jnp.float32),
        in_specs=[hbm] * 8,
        out_specs=vmem,
        scratch_shapes=[
            pltpu.SMEM((2, columns), jnp.int32),
            pltpu.SMEM((2 * steps, columns), jnp.int32),
            pltpu.SMEM(phonon_weight.shape, jnp.float32),
            pltpu.SMEM((energy_count,), jnp.float32),
            pltpu.SMEM((energy_count,), jnp.float32),
            pltpu.VMEM(blocks, jnp.float32),
            pltpu.VMEM(coupling.shape[1:], jnp.float32),
            pltpu.VMEM((1, n), jnp.float32),
            pltpu.VMEM((1, n), jnp.float32),
            pltpu.VMEM((2, 2, n, n), jnp.float32),
            pltpu.VMEM((modes * n // 2, 3 * n), jnp.bfloat16),
            pltpu.VMEM((modes, 3 * n, n), jnp.bfloat16),
            pltpu.VMEM((modes, n, n), jnp.float32),
            pltpu.VMEM((2,) + blocks, jnp.float32),
            pltpu.VMEM((2,) + blocks, jnp.float32),
            pltpu.VMEM(halves, jnp.float32),
            pltpu.VMEM((steps,) + blocks, jnp.float32),
            pltpu.VMEM(blocks, jnp.float32),
            pltpu.VMEM(blocks, jnp.float32),
            pltpu.VMEM((n, n), jnp.float32),
            dma((6,)),
            dma,
            dma((energy_count, 2)),
            dma((2 * steps + 1,)),
            dma((2 * steps + 1,)),
            dma((2, 2)),
            dma((2, 2)),
            dma((energy_count, 2)),
            dma((energy_count, 2)),
            dma((energy_count, 2)),
            dma((energy_count, 2)),
            dma((energy_count, 2, 2 * steps)),
            dma((steps, energy_count, 2, 2)),
            dma((energy_count, pieces)),
            dma((energy_count, pieces)),
        ],
        compiler_params=pltpu.CompilerParams(
            collective_id=0, has_side_effects=True, vmem_limit_bytes=50 << 20
        ),
    )(
        *(
            pltpu.with_memory_space_constraint(value, pltpu.HBM)
            for value in (
                mode_index[0], phonon_weight, energies, guess_scale.reshape(energy_count),
                green.reshape(blocks), coupling[0], onsite, hopping,
            )
        )
    )
    return out.reshape(1, energy_count, 1, 2, n, n)


def solution(mesh):
    placed = (
        P("kz", "en", "sp", None, None, None),
        P("sp", None, None, None),
        P(),
        P("kz", None),
        P("sp", None),
        P("sp", None),
        P("en"),
        P("kz", "en", "sp"),
    )
    sizes = tuple(mesh.shape[axis] for axis in ("kz", "en", "sp"))
    return jax.shard_map(
        functools.partial(body, sizes),
        mesh=mesh,
        in_specs=placed,
        out_specs=P("kz", "en", "sp", None, None, None),
        check_vma=False,
    )
```

```python
import functools

import jax
import jax.numpy as jnp
from jax import lax
from jax.experimental import pallas as pl
from jax.experimental.pallas import tpu as pltpu
from jax.sharding import PartitionSpec as P

REACH = 2
ROW_BLOCKS = 8
TAKEN = (1, 1, 2, 0, 1, 0)
MESH = pl.DeviceIdType.MESH


def split(value):
    high = value.astype(jnp.bfloat16)
    return high, (value - high.astype(jnp.float32)).astype(jnp.bfloat16)


def dot_split(first, second):
    left = jnp.concatenate([first[0], first[0], first[1]], axis=1)
    right = jnp.concatenate([second[0], second[1], second[0]], axis=0)
    return jnp.dot(left, right, preferred_element_type=jnp.float32)


def complex_pair(re, im):
    return jnp.concatenate(
        [jnp.concatenate([re, -im], axis=1), jnp.concatenate([im, re], axis=1)], axis=0
    )


def kernel(
    sizes,
    mode_in, weight_in, energy_in, guess_in, green_in, coupling_in, onsite_in, hopping_in,
    out_ref,
    mode_near, mode_far, weight_ref, energy_ref, guess_ref,
    green_ref, coupling_ref, onsite_ref, hopping_ref,
    halo, left3, right3, terms, blocks, near, message, arrived, inverse, before, outer,
    ready, small_sem, coupling_sem, green_sem, first_sem, mode_send, mode_recv, halo_send, halo_recv,
    block_send, block_recv, near_send, near_recv, kz_send, kz_recv, sp_send, sp_recv,
):
    kz_count, en_count, sp_count = sizes
    energy_count, _, n, _ = green_ref.shape
    modes = coupling_ref.shape[0]
    ring = kz_count > 2 * REACH
    steps = (REACH, -REACH) if ring else (REACH,)
    messages = [(d, t) for d in range(len(steps)) for t in range(2)]
    half = n // 2
    rows = n // ROW_BLOCKS
    pieces = 2 * ROW_BLOCKS
    k, en, sp = lax.axis_index("kz"), lax.axis_index("en"), lax.axis_index("sp")
    odd = lax.rem(k, 2)
    base = k - odd
    sibling = base + 1 - odd

    def far(d, t):
        return lax.rem(base + t + steps[d] + kz_count, kz_count)

    def origin(d, t):
        return lax.rem(base + t - steps[d] + kz_count, kz_count)

    direct = en_count == 2 and energy_count == 2

    def first_load(p):
        return pltpu.make_async_copy(green_in.at[1 - en, p], blocks.at[odd, 0, p],
                                     first_sem.at[p])

    green_load = pltpu.make_async_copy(green_in, green_ref, green_sem)
    coupling_load = pltpu.make_async_copy(coupling_in, coupling_ref, coupling_sem)
    small_loads = [
        pltpu.make_async_copy(source, target, small_sem.at[index])
        for index, (source, target) in enumerate((
            (mode_in, mode_near.at[odd]), (weight_in, weight_ref), (energy_in, energy_ref),
            (guess_in, guess_ref), (onsite_in, onsite_ref), (hopping_in, hopping_ref),
        ))
    ]
    barrier = pltpu.get_barrier_semaphore()

    def greet(axis, index):
        pl.semaphore_signal(barrier, inc=1, device_id={axis: index}, device_id_type=MESH)

    greet("kz", sibling)
    for d, t in messages:
        greet("kz", far(d, t))
    for axis, here, count in (("en", en, en_count), ("sp", sp, sp_count)):
        pl.when(here < count - 1)(lambda axis=axis, here=here: greet(axis, here + 1))
    coupling_load.start()
    if direct:
        for p in range(2):
            first_load(p).start()
    for load in small_loads:
        load.start()
    green_load.start()
    expected = 1 + len(messages)
    for here in (en, sp):
        expected = expected + (here > 0).astype(jnp.int32)
    pl.semaphore_wait(barrier, expected)
    for index, (axis, here) in enumerate((("en", en), ("sp", sp))):
        @pl.when(here > 0)
        def _():
            pl.semaphore_signal(ready.at[index], inc=1, device_id={axis: here - 1},
                                device_id_type=MESH)

    def remote(source, target, send, recv, axis, index):
        return pltpu.make_async_remote_copy(
            src_ref=source, dst_ref=target, send_sem=send, recv_sem=recv,
            device_id={axis: index}, device_id_type=MESH,
        )

    def halo_up(p):
        return remote(green_in.at[energy_count - 1, p], halo.at[0, p],
                      halo_send.at[0], halo_recv.at[0, p], "en", en + 1)

    def halo_down(p):
        return remote(green_in.at[0, p], halo.at[1, p],
                      halo_send.at[1], halo_recv.at[1, p], "en", en - 1)

    def mode_to_sibling(parity):
        return remote(mode_in, mode_near.at[parity], mode_send.at[2 * len(steps)],
                      mode_recv.at[len(messages)], "kz", sibling)

    def mode_to_origin(d, t, slot):
        return remote(mode_in, mode_far.at[2 * d + slot], mode_send.at[2 * d + t],
                      mode_recv.at[2 * d + slot], "kz", origin(d, t))

    def swap(i, p, parity):
        source = green_in.at[1 - en, p] if direct and i == 0 else blocks.at[parity, i, p]
        return remote(source, blocks.at[parity, i, p], block_send, block_recv.at[i, p],
                      "kz", sibling)

    mode_to_sibling(odd).start()
    for d, t in messages:
        mode_to_origin(d, t, odd).start()
    if direct:
        for p in range(2):
            swap(0, p, odd).start()
    for p in range(2):
        pl.when(en > 0)(lambda p=p: halo_down(p).start())

    def start_up():
        @pl.when(en < en_count - 1)
        def _():
            pl.semaphore_wait(ready.at[0], 1)
            for p in range(2):
                halo_up(p).start()


    def energy_of(i):
        return lax.rem(i + en, energy_count)

    def load_block(i, p):
        e = energy_of(i)
        below = green_ref[jnp.maximum(e - 1, 0), p]
        above = green_ref[jnp.minimum(e + 1, energy_count - 1), p]

        @pl.when((e > 0) & (e < energy_count - 1))
        def _():
            blocks[odd, i, p] = below + above

        @pl.when((e == 0) & (en > 0))
        def _():
            halo_up(p).wait_recv()
            blocks[odd, i, p] = halo[0, p] + above

        @pl.when((e == 0) & (en == 0))
        def _():
            blocks[odd, i, p] = above

        @pl.when((e > 0) & (e == energy_count - 1) & (en < en_count - 1))
        def _():
            halo_down(p).wait_recv()
            blocks[odd, i, p] = below + halo[1, p]

        @pl.when((e > 0) & (e == energy_count - 1) & (en == en_count - 1))
        def _():
            blocks[odd, i, p] = below

        swap(i, p, odd).start()

    def columns(d, t, source):
        if source == t:
            if not ring:
                return (2 * REACH, 0)
            return (2 * REACH,) if d == 0 else (0,)
        if not ring or t == d:
            return (2 * REACH - 1,) if t == 0 else (1,)
        return ()

    def picked(row, column, source):
        return terms[row[column], pl.ds(source * half, half)]

    def over(i, p, j, side):
        d, t = messages[j]
        return remote(message.at[i, t, p, d],
                      arrived.at[d, i, p, pl.ds(pl.multiple_of(side * half, half), half)],
                      kz_send.at[i, t], kz_recv.at[i], "kz", far(d, t))

    def near_half(i, p, parity, side):
        at = near.at[parity, i, p, pl.ds(pl.multiple_of(side * half, half), half)]
        return remote(at, at, near_send, near_recv.at[i], "kz", sibling)

    def block_terms(i, p, between=lambda: None):
        between()
        swap(i, p, 1 - odd).wait_recv()
        first = [
            dot_split((left3[:, :n], left3[:, 2 * n:]), split(blocks[source, i, p]))
            for source in range(2)
        ]
        between()
        for m in range(modes):
            at = slice(m * half, (m + 1) * half)
            high, low = split(jnp.concatenate([first[0][at], first[1][at]], axis=0))
            terms[m] = jnp.dot(
                jnp.concatenate([high, high, low], axis=1), right3[m],
                preferred_element_type=jnp.float32,
            )
            between()

    def block_messages(i, p):
        for j, (d, t) in enumerate(messages):
            message[i, t, p, d] = sum(
                picked(mode_far.at[2 * d + t], column, source)
                for source in range(2) for column in columns(d, t, source)
            )
        at = pl.ds(pl.multiple_of(odd * half, half), half)
        for t in range(2):
            near[t, i, p, at] = (
                picked(mode_near.at[t], REACH, t)
                + picked(mode_near.at[t], REACH + 2 * t - 1, 1 - t)
            )
        near_half(i, p, 1 - odd, odd).start()

    def targets(side):
        return [j for j, (d, t) in enumerate(messages) if t == side]

    def send(i, p, side):
        for j in targets(side):
            over(i, p, j, odd).start()

    def drain(i, side):
        whole = message.at[i, side]
        remote(whole, whole, kz_send.at[i, side], kz_recv.at[i], "kz",
               far(0, side)).wait_send()

    def collect(i, p):
        value = near[odd, i, p]
        for d in range(len(steps)):
            value = value + arrived[d, i, p]
        return value

    def place(j):
        block, rest = j // ROW_BLOCKS, lax.rem(j, ROW_BLOCKS)
        p, r = rest // (ROW_BLOCKS // 2), lax.rem(rest, ROW_BLOCKS // 2)
        return p, pl.ds(pl.multiple_of(block * half + r * rows, rows), rows)

    def link(i, j):
        p, at = place(j)
        return remote(out_ref.at[energy_of(i), p, at], before.at[i, p, at],
                      sp_send.at[i], sp_recv.at[i, j], "sp", sp + 1)

    def chain_step(i, j):
        p, at = place(j)
        e = energy_of(i)

        @pl.when(sp > 0)
        def _():
            link(i, j).wait_recv()
            out_ref[e, p, at] = outer[at] * before[i, p, at] + inverse[i, p, at]

        @pl.when(sp == 0)
        def _():
            out_ref[e, p, at] = inverse[i, p, at]

        @pl.when(sp < sp_count - 1)
        def _():
            link(i, j).start()

    early = jnp.clip(pieces - (sp - 1) * (ROW_BLOCKS - 1), 0, pieces)

    def chain_part(i, first, last):
        @pl.loop(first, last)
        def _(j):
            chain_step(i, j)

    def invert(i):
        whole = near.at[odd, i, :, pl.ds(pl.multiple_of((1 - odd) * half, half), half)]
        remote(whole, whole, near_send, near_recv.at[i], "kz", sibling).wait_recv()
        whole = arrived.at[:, i]
        remote(whole, whole, kz_send.at[i, 0], kz_recv.at[i], "kz", far(0, 0)).wait_recv()
        e = energy_of(i)
        guess = guess_ref[e]
        shift = onsite_ref[...] - energy_ref[e]
        diagonal = (lax.broadcasted_iota(jnp.int32, (n, n), 0)
                    == lax.broadcasted_iota(jnp.int32, (n, n), 1))
        r_re = jnp.where(diagonal, 1.0 - guess * shift, 0.0) - guess * collect(i, 0)
        r_im = -guess * collect(i, 1)

        def stack(re, im):
            return tuple(
                jnp.concatenate([a, b], axis=0) for a, b in zip(split(re), split(im))
            )

        def sides(re, im):
            return split(re), split(im), split(re + im)

        def joined(first, second):
            return tuple(jnp.concatenate(pair, axis=0) for pair in zip(first, second))

        def finish(products):
            re, im, both = products
            return re - im, both - re - im

        r_sides = sides(r_re, r_im)
        s_re, s_im = finish([dot_split(side, side) for side in r_sides])
        s_sides = sides(s_re, s_im)
        products = [dot_split(joined(r, s), s) for r, s in zip(r_sides, s_sides)]
        cube = finish([product[:n] for product in products])
        fourth = finish([product[n:] for product in products])
        one = jnp.where(diagonal, 1.0, 0.0)
        p_re = one + r_re + s_re + cube[0]
        p_im = r_im + s_im + cube[1]
        re, im = split(p_re), split(p_im)
        fourth = stack(*fourth)
        for block in range(2):
            at = slice(block * half, (block + 1) * half)
            rows_left = tuple(complex_pair(a[at], b[at]) for a, b in zip(re, im))
            result = dot_split(rows_left, fourth)
            inverse[i, 0, at] = guess * (p_re[at] + result[:half])
            inverse[i, 1, at] = guess * (p_im[at] + result[half:])
            pl.when(sp == 0)(lambda: chain_part(i, block * ROW_BLOCKS, (block + 1) * ROW_BLOCKS))

    if not direct:
        start_up()
        green_load.wait()
        for p in range(2):
            load_block(0, p)
    for load in small_loads:
        load.wait()
    coupling_load.wait()
    for m in range(modes):
        at = slice(m * half, (m + 1) * half)
        here = pl.ds(pl.multiple_of(odd * half, half), half)
        high, low = split(coupling_ref[m, here])
        left3[at] = jnp.concatenate([high, high, low], axis=1)
        high, low = split(coupling_ref[m].T * weight_ref[m])
        right3[m] = jnp.concatenate([high, low, high], axis=0)
    if direct:
        start_up()
        for p in range(2):
            first_load(p).wait()
    block_terms(0, 0)
    mode_to_sibling(1 - odd).wait_recv()
    for d, t in messages:
        mode_to_origin(d, t, t).wait_recv()
    block_messages(0, 0)
    send(0, 0, 0)
    block_terms(0, 1)
    block_messages(0, 1)
    send(0, 1, 0)
    across = jnp.broadcast_to(hopping_ref[...], (n, n))
    outer[...] = across * across.T

    @pl.when(sp < sp_count - 1)
    def _():
        pl.semaphore_wait(ready.at[1], 1)

    if direct:
        green_load.wait()
    if energy_count > 1:
        load_block(1, 0)
    drain(0, 0)
    for p in range(2):
        send(0, p, 1)

    for i in range(energy_count):
        last = i == energy_count - 1

        def second(i=i, between=lambda: None):
            load_block(i + 1, 1)
            between()
            drain(i, 1)
            send(i + 1, 0, 0)
            block_terms(i + 1, 1, between)
            block_messages(i + 1, 1)
            send(i + 1, 1, 0)

        def turn(i=i):
            drain(i + 1, 0)
            for p in range(2):
                send(i + 1, p, 1)

        if last:
            invert(i)
            drain(i, 1)
            pl.when(sp > 0)(lambda i=i: chain_part(i, 0, pieces))
            continue
        if i > 0:
            load_block(i + 1, 0)
        block_terms(i + 1, 0)
        block_messages(i + 1, 0)
        pl.when(odd == 1)(second)
        invert(i)

        @pl.when(odd == 0)
        def _():
            taken = []

            def between():
                step = len(taken)
                taken.append(TAKEN[step] if step < len(TAKEN) else 0)
                first, end = sum(taken[:step]), sum(taken)
                if first < end:
                    pl.when(sp == 1)(lambda: chain_part(i, first, end))

            second(between=between)
            begun = jnp.where(sp == 1, sum(taken), 0)
            pl.when(sp > 0)(lambda: chain_part(i, begun, early))
            turn()
            pl.when(sp > 0)(lambda: chain_part(i, early, pieces))

        @pl.when(odd == 1)
        def _():
            turn()
            pl.when(sp > 0)(lambda: chain_part(i, 0, pieces))

    mode_to_sibling(odd).wait_send()
    for d, t in messages:
        mode_to_origin(d, t, odd).wait_send()
    @pl.when(en < en_count - 1)
    def _():
        remote(green_in.at[energy_count - 1], halo.at[0], halo_send.at[0], halo_recv.at[0, 0],
               "en", en + 1).wait_send()

    @pl.when(en > 0)
    def _():
        remote(green_in.at[0], halo.at[1], halo_send.at[1], halo_recv.at[1, 0],
               "en", en - 1).wait_send()

    whole = blocks.at[odd]
    remote(whole, whole, block_send, block_recv.at[0, 0], "kz", sibling).wait_send()
    whole = near.at[1 - odd, :, :, pl.ds(pl.multiple_of(odd * half, half), half)]
    remote(whole, whole, near_send, near_recv.at[0], "kz", sibling).wait_send()

    @pl.when(sp < sp_count - 1)
    def _():
        for i in range(energy_count):
            remote(out_ref.at[energy_of(i)], before.at[i], sp_send.at[i], sp_recv.at[i, 0],
                   "sp", sp + 1).wait_send()


def body(sizes, green, coupling, phonon_weight, mode_index, onsite, hopping, energies, guess_scale):
    energy_count, n = green.shape[1], green.shape[-1]
    modes = coupling.shape[1]
    blocks = (energy_count, 2, n, n)
    steps = 2 if sizes[0] > 2 * REACH else 1
    halves = (energy_count, 2, 2, steps, n // 2, n)
    pieces = 2 * ROW_BLOCKS
    hbm = pl.BlockSpec(memory_space=pltpu.HBM)
    vmem = pl.BlockSpec(memory_space=pltpu.VMEM)
    columns = mode_index.shape[1]
    dma = pltpu.SemaphoreType.DMA
    out = pl.pallas_call(
        functools.partial(kernel, sizes),
        out_shape=jax.ShapeDtypeStruct(blocks, jnp.float32),
        in_specs=[hbm] * 8,
        out_specs=vmem,
        scratch_shapes=[
            pltpu.SMEM((2, columns), jnp.int32),
            pltpu.SMEM((2 * steps, columns), jnp.int32),
            pltpu.SMEM(phonon_weight.shape, jnp.float32),
            pltpu.SMEM((energy_count,), jnp.float32),
            pltpu.SMEM((energy_count,), jnp.float32),
            pltpu.VMEM(blocks, jnp.float32),
            pltpu.VMEM(coupling.shape[1:], jnp.float32),
            pltpu.VMEM((1, n), jnp.float32),
            pltpu.VMEM((1, n), jnp.float32),
            pltpu.VMEM((2, 2, n, n), jnp.float32),
            pltpu.VMEM((modes * n // 2, 3 * n), jnp.bfloat16),
            pltpu.VMEM((modes, 3 * n, n), jnp.bfloat16),
            pltpu.VMEM((modes, n, n), jnp.float32),
            pltpu.VMEM((2,) + blocks, jnp.float32),
            pltpu.VMEM((2,) + blocks, jnp.float32),
            pltpu.VMEM(halves, jnp.float32),
            pltpu.VMEM((steps,) + blocks, jnp.float32),
            pltpu.VMEM(blocks, jnp.float32),
            pltpu.VMEM(blocks, jnp.float32),
            pltpu.VMEM((n, n), jnp.float32),
            pltpu.SemaphoreType.REGULAR((2,)),
            dma((6,)),
            dma,
            dma,
            dma((2,)),
            dma((2 * steps + 1,)),
            dma((2 * steps + 1,)),
            dma((2,)),
            dma((2, 2)),
            dma,
            dma((energy_count, 2)),
            dma,
            dma((energy_count,)),
            dma((energy_count, 2)),
            dma((energy_count,)),
            dma((energy_count,)),
            dma((energy_count, pieces)),
        ],
        compiler_params=pltpu.CompilerParams(
            collective_id=0, has_side_effects=True, vmem_limit_bytes=50 << 20
        ),
    )(
        *(
            pltpu.with_memory_space_constraint(value, pltpu.HBM)
            for value in (
                mode_index[0], phonon_weight, energies, guess_scale.reshape(energy_count),
                green.reshape(blocks), coupling[0], onsite, hopping,
            )
        )
    )
    return out.reshape(1, energy_count, 1, 2, n, n)


def solution(mesh):
    placed = (
        P("kz", "en", "sp", None, None, None),
        P("sp", None, None, None),
        P(),
        P("kz", None),
        P("sp", None),
        P("sp", None),
        P("en"),
        P("kz", "en", "sp"),
    )
    sizes = tuple(mesh.shape[axis] for axis in ("kz", "en", "sp"))
    return jax.shard_map(
        functools.partial(body, sizes),
        mesh=mesh,
        in_specs=placed,
        out_specs=P("kz", "en", "sp", None, None, None),
        check_vma=False,
    )
```

```python
import functools

import jax
import jax.numpy as jnp
from jax import lax
from jax.experimental import pallas as pl
from jax.experimental.pallas import tpu as pltpu
from jax.sharding import PartitionSpec as P

REACH = 2
ROW_BLOCKS = 8
TAKEN = (1, 1, 2, 1, 0, 1)
MESH = pl.DeviceIdType.MESH


def split(value):
    high = value.astype(jnp.bfloat16)
    return high, (value - high.astype(jnp.float32)).astype(jnp.bfloat16)


def dot_split(first, second):
    left = jnp.concatenate([first[0], first[0], first[1]], axis=1)
    right = jnp.concatenate([second[0], second[1], second[0]], axis=0)
    return jnp.dot(left, right, preferred_element_type=jnp.float32)


def complex_pair(re, im):
    return jnp.concatenate(
        [jnp.concatenate([re, -im], axis=1), jnp.concatenate([im, re], axis=1)], axis=0
    )


def kernel(
    sizes,
    mode_in, weight_in, energy_in, guess_in, green_in, coupling_in, onsite_in, hopping_in,
    out_ref,
    mode_near, mode_far, weight_ref, energy_ref, guess_ref,
    green_ref, coupling_ref, onsite_ref, hopping_ref,
    halo, left3, right3, terms, blocks, near, message, arrived, inverse, before, outer,
    ready, small_sem, coupling_sem, green_sem, first_sem, mode_send, mode_recv, halo_send, halo_recv,
    block_send, block_recv, near_send, near_recv, kz_send, kz_recv, sp_send, sp_recv,
):
    kz_count, en_count, sp_count = sizes
    energy_count, _, n, _ = green_ref.shape
    modes = coupling_ref.shape[0]
    ring = kz_count > 2 * REACH
    steps = (REACH, -REACH) if ring else (REACH,)
    messages = [(d, t) for d in range(len(steps)) for t in range(2)]
    half = n // 2
    rows = n // ROW_BLOCKS
    pieces = 2 * ROW_BLOCKS
    k, en, sp = lax.axis_index("kz"), lax.axis_index("en"), lax.axis_index("sp")
    odd = lax.rem(k, 2)
    base = k - odd
    sibling = base + 1 - odd

    def far(d, t):
        return lax.rem(base + t + steps[d] + kz_count, kz_count)

    def origin(d, t):
        return lax.rem(base + t - steps[d] + kz_count, kz_count)

    direct = en_count == 2 and energy_count == 2

    def first_load(p):
        return pltpu.make_async_copy(green_in.at[1 - en, p], blocks.at[odd, 0, p],
                                     first_sem.at[p])

    green_load = pltpu.make_async_copy(green_in, green_ref, green_sem)
    coupling_load = pltpu.make_async_copy(coupling_in, coupling_ref, coupling_sem)
    small_loads = [
        pltpu.make_async_copy(source, target, small_sem.at[index])
        for index, (source, target) in enumerate((
            (mode_in, mode_near.at[odd]), (weight_in, weight_ref), (energy_in, energy_ref),
            (guess_in, guess_ref), (onsite_in, onsite_ref), (hopping_in, hopping_ref),
        ))
    ]
    barrier = pltpu.get_barrier_semaphore()

    def greet(axis, index):
        pl.semaphore_signal(barrier, inc=1, device_id={axis: index}, device_id_type=MESH)

    greet("kz", sibling)
    for d, t in messages:
        greet("kz", far(d, t))
    for axis, here, count in (("en", en, en_count), ("sp", sp, sp_count)):
        pl.when(here < count - 1)(lambda axis=axis, here=here: greet(axis, here + 1))
    coupling_load.start()
    if direct:
        for p in range(2):
            first_load(p).start()
    for load in small_loads:
        load.start()
    green_load.start()
    expected = 1 + len(messages)
    for here in (en, sp):
        expected = expected + (here > 0).astype(jnp.int32)
    pl.semaphore_wait(barrier, expected)
    for index, (axis, here) in enumerate((("en", en), ("sp", sp))):
        @pl.when(here > 0)
        def _():
            pl.semaphore_signal(ready.at[index], inc=1, device_id={axis: here - 1},
                                device_id_type=MESH)

    def remote(source, target, send, recv, axis, index):
        return pltpu.make_async_remote_copy(
            src_ref=source, dst_ref=target, send_sem=send, recv_sem=recv,
            device_id={axis: index}, device_id_type=MESH,
        )

    def halo_up(p):
        return remote(green_in.at[energy_count - 1, p], halo.at[0, p],
                      halo_send.at[0], halo_recv.at[0, p], "en", en + 1)

    def halo_down(p):
        return remote(green_in.at[0, p], halo.at[1, p],
                      halo_send.at[1], halo_recv.at[1, p], "en", en - 1)

    def mode_to_sibling(parity):
        return remote(mode_in, mode_near.at[parity], mode_send.at[2 * len(steps)],
                      mode_recv.at[len(messages)], "kz", sibling)

    def mode_to_origin(d, t, slot):
        return remote(mode_in, mode_far.at[2 * d + slot], mode_send.at[2 * d + t],
                      mode_recv.at[2 * d + slot], "kz", origin(d, t))

    def swap(i, p, parity):
        source = green_in.at[1 - en, p] if direct and i == 0 else blocks.at[parity, i, p]
        return remote(source, blocks.at[parity, i, p], block_send, block_recv.at[i, p],
                      "kz", sibling)

    mode_to_sibling(odd).start()
    for d, t in messages:
        mode_to_origin(d, t, odd).start()
    if direct:
        for p in range(2):
            swap(0, p, odd).start()
    for p in range(2):
        pl.when(en > 0)(lambda p=p: halo_down(p).start())

    def start_up():
        @pl.when(en < en_count - 1)
        def _():
            pl.semaphore_wait(ready.at[0], 1)
            for p in range(2):
                halo_up(p).start()


    def energy_of(i):
        return lax.rem(i + en, energy_count)

    def load_block(i, p):
        e = energy_of(i)
        below = green_ref[jnp.maximum(e - 1, 0), p]
        above = green_ref[jnp.minimum(e + 1, energy_count - 1), p]

        @pl.when((e > 0) & (e < energy_count - 1))
        def _():
            blocks[odd, i, p] = below + above

        @pl.when((e == 0) & (en > 0))
        def _():
            halo_up(p).wait_recv()
            blocks[odd, i, p] = halo[0, p] + above

        @pl.when((e == 0) & (en == 0))
        def _():
            blocks[odd, i, p] = above

        @pl.when((e > 0) & (e == energy_count - 1) & (en < en_count - 1))
        def _():
            halo_down(p).wait_recv()
            blocks[odd, i, p] = below + halo[1, p]

        @pl.when((e > 0) & (e == energy_count - 1) & (en == en_count - 1))
        def _():
            blocks[odd, i, p] = below

        swap(i, p, odd).start()

    def columns(d, t, source):
        if source == t:
            if not ring:
                return (2 * REACH, 0)
            return (2 * REACH,) if d == 0 else (0,)
        if not ring or t == d:
            return (2 * REACH - 1,) if t == 0 else (1,)
        return ()

    def picked(row, column, source):
        other = 1 - odd if source else odd
        return terms[row[column], pl.ds(pl.multiple_of(other * half, half), half)]

    def over(i, p, j, side):
        d, t = messages[j]
        return remote(message.at[i, t, p, d],
                      arrived.at[d, i, p, pl.ds(pl.multiple_of(side * half, half), half)],
                      kz_send.at[i, t], kz_recv.at[i], "kz", far(d, t))

    def near_half(i, p, parity, side):
        at = near.at[parity, i, p, pl.ds(pl.multiple_of(side * half, half), half)]
        return remote(at, at, near_send, near_recv.at[i], "kz", sibling)

    def block_terms(i, p, between=lambda: None, gate=None):
        def product(parity):
            return dot_split((left3[:, :n], left3[:, 2 * n:]), split(blocks[parity, i, p]))

        if gate is None:
            swap(i, p, 1 - odd).wait_recv()
            first = [product(odd), product(1 - odd)]
        else:
            first = [product(odd)]
            between()
            gate()
            between()
            swap(i, p, 1 - odd).wait_recv()
            first.append(product(1 - odd))
        between()
        for m in range(modes):
            at = slice(m * half, (m + 1) * half)
            high, low = split(jnp.concatenate([first[0][at], first[1][at]], axis=0))
            terms[m] = jnp.dot(
                jnp.concatenate([high, high, low], axis=1), right3[m],
                preferred_element_type=jnp.float32,
            )
            between()

    def block_messages(i, p):
        for j, (d, t) in enumerate(messages):
            message[i, t, p, d] = sum(
                picked(mode_far.at[2 * d + t], column, source)
                for source in range(2) for column in columns(d, t, source)
            )
        at = pl.ds(pl.multiple_of(odd * half, half), half)
        for t in range(2):
            near[t, i, p, at] = (
                picked(mode_near.at[t], REACH, t)
                + picked(mode_near.at[t], REACH + 2 * t - 1, 1 - t)
            )
        near_half(i, p, 1 - odd, odd).start()

    def targets(side):
        return [j for j, (d, t) in enumerate(messages) if t == side]

    def send(i, p, side):
        for j in targets(side):
            over(i, p, j, odd).start()

    def drain(i, side):
        whole = message.at[i, side]
        remote(whole, whole, kz_send.at[i, side], kz_recv.at[i], "kz",
               far(0, side)).wait_send()

    def collect(i, p):
        value = near[odd, i, p]
        for d in range(len(steps)):
            value = value + arrived[d, i, p]
        return value

    def place(j):
        block, rest = j // ROW_BLOCKS, lax.rem(j, ROW_BLOCKS)
        p, r = rest // (ROW_BLOCKS // 2), lax.rem(rest, ROW_BLOCKS // 2)
        return p, pl.ds(pl.multiple_of(block * half + r * rows, rows), rows)

    def link(i, j):
        p, at = place(j)
        return remote(out_ref.at[energy_of(i), p, at], before.at[i, p, at],
                      sp_send.at[i], sp_recv.at[i, j], "sp", sp + 1)

    def chain_step(i, j):
        p, at = place(j)
        e = energy_of(i)

        @pl.when(sp > 0)
        def _():
            link(i, j).wait_recv()
            out_ref[e, p, at] = outer[at] * before[i, p, at] + inverse[i, p, at]

        @pl.when(sp == 0)
        def _():
            out_ref[e, p, at] = inverse[i, p, at]

        @pl.when(sp < sp_count - 1)
        def _():
            link(i, j).start()

    early = jnp.clip(pieces - (sp - 1) * (ROW_BLOCKS - 1), 0, pieces)

    def chain_part(i, first, last):
        @pl.loop(first, last)
        def _(j):
            chain_step(i, j)

    def invert(i):
        whole = near.at[odd, i, :, pl.ds(pl.multiple_of((1 - odd) * half, half), half)]
        remote(whole, whole, near_send, near_recv.at[i], "kz", sibling).wait_recv()
        whole = arrived.at[:, i]
        remote(whole, whole, kz_send.at[i, 0], kz_recv.at[i], "kz", far(0, 0)).wait_recv()
        e = energy_of(i)
        guess = guess_ref[e]
        shift = onsite_ref[...] - energy_ref[e]
        diagonal = (lax.broadcasted_iota(jnp.int32, (n, n), 0)
                    == lax.broadcasted_iota(jnp.int32, (n, n), 1))
        r_re = jnp.where(diagonal, 1.0 - guess * shift, 0.0) - guess * collect(i, 0)
        r_im = -guess * collect(i, 1)

        def stack(re, im):
            return tuple(
                jnp.concatenate([a, b], axis=0) for a, b in zip(split(re), split(im))
            )

        def sides(re, im):
            return split(re), split(im), split(re + im)

        def joined(first, second):
            return tuple(jnp.concatenate(pair, axis=0) for pair in zip(first, second))

        def finish(products):
            re, im, both = products
            return re - im, both - re - im

        r_sides = sides(r_re, r_im)
        s_re, s_im = finish([dot_split(side, side) for side in r_sides])
        s_sides = sides(s_re, s_im)
        products = [dot_split(joined(r, s), s) for r, s in zip(r_sides, s_sides)]
        cube = finish([product[:n] for product in products])
        fourth = finish([product[n:] for product in products])
        one = jnp.where(diagonal, 1.0, 0.0)
        p_re = one + r_re + s_re + cube[0]
        p_im = r_im + s_im + cube[1]
        re, im = split(p_re), split(p_im)
        fourth = stack(*fourth)
        for block in range(2):
            at = slice(block * half, (block + 1) * half)
            rows_left = tuple(complex_pair(a[at], b[at]) for a, b in zip(re, im))
            result = dot_split(rows_left, fourth)
            inverse[i, 0, at] = guess * (p_re[at] + result[:half])
            inverse[i, 1, at] = guess * (p_im[at] + result[half:])
            pl.when(sp == 0)(lambda: chain_part(i, block * ROW_BLOCKS, (block + 1) * ROW_BLOCKS))

    if not direct:
        start_up()
        green_load.wait()
        for p in range(2):
            load_block(0, p)
    for load in small_loads:
        load.wait()
    coupling_load.wait()
    for m in range(modes):
        at = slice(m * half, (m + 1) * half)
        here = pl.ds(pl.multiple_of(odd * half, half), half)
        high, low = split(coupling_ref[m, here])
        left3[at] = jnp.concatenate([high, high, low], axis=1)
        high, low = split(coupling_ref[m].T * weight_ref[m])
        right3[m] = jnp.concatenate([high, low, high], axis=0)
    if direct:
        start_up()
        for p in range(2):
            first_load(p).wait()
    block_terms(0, 0)
    mode_to_sibling(1 - odd).wait_recv()
    for d, t in messages:
        mode_to_origin(d, t, t).wait_recv()
    block_messages(0, 0)
    send(0, 0, 0)
    block_terms(0, 1)
    block_messages(0, 1)
    send(0, 1, 0)
    across = jnp.broadcast_to(hopping_ref[...], (n, n))
    outer[...] = across * across.T

    @pl.when(sp < sp_count - 1)
    def _():
        pl.semaphore_wait(ready.at[1], 1)

    if direct:
        green_load.wait()
    if energy_count > 1:
        load_block(1, 0)
    drain(0, 0)
    for p in range(2):
        send(0, p, 1)

    for i in range(energy_count):
        last = i == energy_count - 1

        def second(i=i, between=lambda: None):
            load_block(i + 1, 1)

            def gate():
                drain(i, 1)
                send(i + 1, 0, 0)

            block_terms(i + 1, 1, between, gate)
            block_messages(i + 1, 1)
            send(i + 1, 1, 0)

        def turn(i=i):
            drain(i + 1, 0)
            for p in range(2):
                send(i + 1, p, 1)

        if last:
            invert(i)
            drain(i, 1)
            pl.when(sp > 0)(lambda i=i: chain_part(i, 0, pieces))
            continue
        if i > 0:
            load_block(i + 1, 0)
        block_terms(i + 1, 0)
        block_messages(i + 1, 0)
        pl.when(odd == 1)(second)
        invert(i)

        @pl.when(odd == 0)
        def _():
            taken = []

            def between():
                step = len(taken)
                taken.append(TAKEN[step] if step < len(TAKEN) else 0)
                first, end = sum(taken[:step]), sum(taken)
                if first < end:
                    pl.when(sp == 1)(lambda: chain_part(i, first, end))

            second(between=between)
            begun = jnp.where(sp == 1, sum(taken), 0)
            pl.when(sp > 0)(lambda: chain_part(i, begun, early))
            turn()
            pl.when(sp > 0)(lambda: chain_part(i, early, pieces))

        @pl.when(odd == 1)
        def _():
            turn()
            pl.when(sp > 0)(lambda: chain_part(i, 0, pieces))

    mode_to_sibling(odd).wait_send()
    for d, t in messages:
        mode_to_origin(d, t, odd).wait_send()
    @pl.when(en < en_count - 1)
    def _():
        remote(green_in.at[energy_count - 1], halo.at[0], halo_send.at[0], halo_recv.at[0, 0],
               "en", en + 1).wait_send()

    @pl.when(en > 0)
    def _():
        remote(green_in.at[0], halo.at[1], halo_send.at[1], halo_recv.at[1, 0],
               "en", en - 1).wait_send()

    whole = blocks.at[odd]
    remote(whole, whole, block_send, block_recv.at[0, 0], "kz", sibling).wait_send()
    whole = near.at[1 - odd, :, :, pl.ds(pl.multiple_of(odd * half, half), half)]
    remote(whole, whole, near_send, near_recv.at[0], "kz", sibling).wait_send()

    @pl.when(sp < sp_count - 1)
    def _():
        for i in range(energy_count):
            remote(out_ref.at[energy_of(i)], before.at[i], sp_send.at[i], sp_recv.at[i, 0],
                   "sp", sp + 1).wait_send()


def body(sizes, green, coupling, phonon_weight, mode_index, onsite, hopping, energies, guess_scale):
    energy_count, n = green.shape[1], green.shape[-1]
    modes = coupling.shape[1]
    blocks = (energy_count, 2, n, n)
    steps = 2 if sizes[0] > 2 * REACH else 1
    halves = (energy_count, 2, 2, steps, n // 2, n)
    pieces = 2 * ROW_BLOCKS
    hbm = pl.BlockSpec(memory_space=pltpu.HBM)
    vmem = pl.BlockSpec(memory_space=pltpu.VMEM)
    columns = mode_index.shape[1]
    dma = pltpu.SemaphoreType.DMA
    out = pl.pallas_call(
        functools.partial(kernel, sizes),
        out_shape=jax.ShapeDtypeStruct(blocks, jnp.float32),
        in_specs=[hbm] * 8,
        out_specs=vmem,
        scratch_shapes=[
            pltpu.SMEM((2, columns), jnp.int32),
            pltpu.SMEM((2 * steps, columns), jnp.int32),
            pltpu.SMEM(phonon_weight.shape, jnp.float32),
            pltpu.SMEM((energy_count,), jnp.float32),
            pltpu.SMEM((energy_count,), jnp.float32),
            pltpu.VMEM(blocks, jnp.float32),
            pltpu.VMEM(coupling.shape[1:], jnp.float32),
            pltpu.VMEM((1, n), jnp.float32),
            pltpu.VMEM((1, n), jnp.float32),
            pltpu.VMEM((2, 2, n, n), jnp.float32),
            pltpu.VMEM((modes * n // 2, 3 * n), jnp.bfloat16),
            pltpu.VMEM((modes, 3 * n, n), jnp.bfloat16),
            pltpu.VMEM((modes, n, n), jnp.float32),
            pltpu.VMEM((2,) + blocks, jnp.float32),
            pltpu.VMEM((2,) + blocks, jnp.float32),
            pltpu.VMEM(halves, jnp.float32),
            pltpu.VMEM((steps,) + blocks, jnp.float32),
            pltpu.VMEM(blocks, jnp.float32),
            pltpu.VMEM(blocks, jnp.float32),
            pltpu.VMEM((n, n), jnp.float32),
            pltpu.SemaphoreType.REGULAR((2,)),
            dma((6,)),
            dma,
            dma,
            dma((2,)),
            dma((2 * steps + 1,)),
            dma((2 * steps + 1,)),
            dma((2,)),
            dma((2, 2)),
            dma,
            dma((energy_count, 2)),
            dma,
            dma((energy_count,)),
            dma((energy_count, 2)),
            dma((energy_count,)),
            dma((energy_count,)),
            dma((energy_count, pieces)),
        ],
        compiler_params=pltpu.CompilerParams(
            collective_id=0, has_side_effects=True, vmem_limit_bytes=50 << 20
        ),
    )(
        *(
            pltpu.with_memory_space_constraint(value, pltpu.HBM)
            for value in (
                mode_index[0], phonon_weight, energies, guess_scale.reshape(energy_count),
                green.reshape(blocks), coupling[0], onsite, hopping,
            )
        )
    )
    return out.reshape(1, energy_count, 1, 2, n, n)


def solution(mesh):
    placed = (
        P("kz", "en", "sp", None, None, None),
        P("sp", None, None, None),
        P(),
        P("kz", None),
        P("sp", None),
        P("sp", None),
        P("en"),
        P("kz", "en", "sp"),
    )
    sizes = tuple(mesh.shape[axis] for axis in ("kz", "en", "sp"))
    return jax.shard_map(
        functools.partial(body, sizes),
        mesh=mesh,
        in_specs=placed,
        out_specs=P("kz", "en", "sp", None, None, None),
        check_vma=False,
    )
```

```python
import functools

import jax
import jax.numpy as jnp
from jax import lax
from jax.experimental import pallas as pl
from jax.experimental.pallas import tpu as pltpu
from jax.sharding import PartitionSpec as P

REACH = 2
ROW_BLOCKS = 8
PARTS = 4
CUTS = ((0, 1), (1, 4))
TAKEN = (1, 1, 2, 1, 0, 1)
MESH = pl.DeviceIdType.MESH


def split(value):
    high = value.astype(jnp.bfloat16)
    return high, (value - high.astype(jnp.float32)).astype(jnp.bfloat16)


def dot_split(first, second):
    left = jnp.concatenate([first[0], first[0], first[1]], axis=1)
    right = jnp.concatenate([second[0], second[1], second[0]], axis=0)
    return jnp.dot(left, right, preferred_element_type=jnp.float32)


def complex_pair(re, im):
    return jnp.concatenate(
        [jnp.concatenate([re, -im], axis=1), jnp.concatenate([im, re], axis=1)], axis=0
    )


def kernel(
    sizes,
    mode_in, weight_in, energy_in, guess_in, green_in, coupling_in, onsite_in, hopping_in,
    out_ref,
    mode_near, mode_far, weight_ref, energy_ref, guess_ref,
    green_ref, coupling_ref, onsite_ref, hopping_ref,
    halo, left3, right3, terms, blocks, near, message, arrived, inverse, before, outer,
    ready, small_sem, coupling_sem, green_sem, first_sem, mode_send, mode_recv, halo_send, halo_recv,
    block_send, block_recv, near_send, near_recv, kz_send, kz_recv, sp_send, sp_recv,
):
    kz_count, en_count, sp_count = sizes
    energy_count, _, n, _ = green_ref.shape
    modes = coupling_ref.shape[0]
    ring = kz_count > 2 * REACH
    steps = (REACH, -REACH) if ring else (REACH,)
    messages = [(d, t) for d in range(len(steps)) for t in range(2)]
    half = n // 2
    rows = n // ROW_BLOCKS
    pieces = 2 * ROW_BLOCKS
    k, en, sp = lax.axis_index("kz"), lax.axis_index("en"), lax.axis_index("sp")
    odd = lax.rem(k, 2)
    base = k - odd
    sibling = base + 1 - odd

    def far(d, t):
        return lax.rem(base + t + steps[d] + kz_count, kz_count)

    def origin(d, t):
        return lax.rem(base + t - steps[d] + kz_count, kz_count)

    direct = en_count == 2 and energy_count == 2

    def first_load(p):
        return pltpu.make_async_copy(green_in.at[1 - en, p], blocks.at[odd, 0, p],
                                     first_sem.at[p])

    green_load = pltpu.make_async_copy(green_in, green_ref, green_sem)
    coupling_load = pltpu.make_async_copy(coupling_in, coupling_ref, coupling_sem)
    small_loads = [
        pltpu.make_async_copy(source, target, small_sem.at[index])
        for index, (source, target) in enumerate((
            (mode_in, mode_near.at[odd]), (weight_in, weight_ref), (energy_in, energy_ref),
            (guess_in, guess_ref), (onsite_in, onsite_ref), (hopping_in, hopping_ref),
        ))
    ]
    barrier = pltpu.get_barrier_semaphore()

    def greet(axis, index):
        pl.semaphore_signal(barrier, inc=1, device_id={axis: index}, device_id_type=MESH)

    greet("kz", sibling)
    for d, t in messages:
        greet("kz", far(d, t))
    for axis, here, count in (("en", en, en_count), ("sp", sp, sp_count)):
        pl.when(here < count - 1)(lambda axis=axis, here=here: greet(axis, here + 1))
    coupling_load.start()
    if direct:
        for p in range(2):
            first_load(p).start()
    for load in small_loads:
        load.start()
    green_load.start()
    expected = 1 + len(messages)
    for here in (en, sp):
        expected = expected + (here > 0).astype(jnp.int32)
    pl.semaphore_wait(barrier, expected)
    for index, (axis, here) in enumerate((("en", en), ("sp", sp))):
        @pl.when(here > 0)
        def _():
            pl.semaphore_signal(ready.at[index], inc=1, device_id={axis: here - 1},
                                device_id_type=MESH)

    def remote(source, target, send, recv, axis, index):
        return pltpu.make_async_remote_copy(
            src_ref=source, dst_ref=target, send_sem=send, recv_sem=recv,
            device_id={axis: index}, device_id_type=MESH,
        )

    def halo_up(p):
        return remote(green_in.at[energy_count - 1, p], halo.at[0, p],
                      halo_send.at[0], halo_recv.at[0, p], "en", en + 1)

    def halo_down(p):
        return remote(green_in.at[0, p], halo.at[1, p],
                      halo_send.at[1], halo_recv.at[1, p], "en", en - 1)

    def mode_to_sibling(parity):
        return remote(mode_in, mode_near.at[parity], mode_send.at[2 * len(steps)],
                      mode_recv.at[len(messages)], "kz", sibling)

    def mode_to_origin(d, t, slot):
        return remote(mode_in, mode_far.at[2 * d + slot], mode_send.at[2 * d + t],
                      mode_recv.at[2 * d + slot], "kz", origin(d, t))

    def swap(i, p, parity):
        source = green_in.at[1 - en, p] if direct and i == 0 else blocks.at[parity, i, p]
        return remote(source, blocks.at[parity, i, p], block_send, block_recv.at[i, p],
                      "kz", sibling)

    for d, t in messages:
        mode_to_origin(d, t, odd).start()
    mode_to_sibling(odd).start()
    if direct:
        for p in range(2):
            swap(0, p, odd).start()
    for p in range(2):
        pl.when(en > 0)(lambda p=p: halo_down(p).start())

    def start_up():
        @pl.when(en < en_count - 1)
        def _():
            pl.semaphore_wait(ready.at[0], 1)
            for p in range(2):
                halo_up(p).start()


    def energy_of(i):
        return lax.rem(i + en, energy_count)

    def load_block(i, p):
        e = energy_of(i)
        below = green_ref[jnp.maximum(e - 1, 0), p]
        above = green_ref[jnp.minimum(e + 1, energy_count - 1), p]

        @pl.when((e > 0) & (e < energy_count - 1))
        def _():
            blocks[odd, i, p] = below + above

        @pl.when((e == 0) & (en > 0))
        def _():
            halo_up(p).wait_recv()
            blocks[odd, i, p] = halo[0, p] + above

        @pl.when((e == 0) & (en == 0))
        def _():
            blocks[odd, i, p] = above

        @pl.when((e > 0) & (e == energy_count - 1) & (en < en_count - 1))
        def _():
            halo_down(p).wait_recv()
            blocks[odd, i, p] = below + halo[1, p]

        @pl.when((e > 0) & (e == energy_count - 1) & (en == en_count - 1))
        def _():
            blocks[odd, i, p] = below

        swap(i, p, odd).start()

    def columns(d, t, source):
        if source == t:
            if not ring:
                return (2 * REACH, 0)
            return (2 * REACH,) if d == 0 else (0,)
        if not ring or t == d:
            return (2 * REACH - 1,) if t == 0 else (1,)
        return ()

    def picked(row, column, source):
        other = 1 - odd if source else odd
        return terms[row[column], pl.ds(pl.multiple_of(other * half, half), half)]

    def over(i, p, j, side):
        d, t = messages[j]
        return remote(message.at[i, t, p, d],
                      arrived.at[d, i, p, pl.ds(pl.multiple_of(side * half, half), half)],
                      kz_send.at[i, t], kz_recv.at[i], "kz", far(d, t))

    def near_half(i, p, parity, side):
        at = near.at[parity, i, p, pl.ds(pl.multiple_of(side * half, half), half)]
        return remote(at, at, near_send, near_recv.at[i], "kz", sibling)

    def block_terms(i, p, between=lambda: None, gate=None):
        def product(parity):
            return dot_split((left3[:, :n], left3[:, 2 * n:]), split(blocks[parity, i, p]))

        if gate is None:
            swap(i, p, 1 - odd).wait_recv()
            first = [product(odd), product(1 - odd)]
        else:
            first = [product(odd)]
            between()
            gate()
            between()
            swap(i, p, 1 - odd).wait_recv()
            first.append(product(1 - odd))
        between()
        for m in range(modes):
            at = slice(m * half, (m + 1) * half)
            high, low = split(jnp.concatenate([first[0][at], first[1][at]], axis=0))
            terms[m] = jnp.dot(
                jnp.concatenate([high, high, low], axis=1), right3[m],
                preferred_element_type=jnp.float32,
            )
            between()

    def form(i, p, side):
        for d, t in messages:
            if t == side:
                message[i, t, p, d] = sum(
                    picked(mode_far.at[2 * d + t], column, source)
                    for source in range(2) for column in columns(d, t, source)
                )

    def block_messages(i, p, sides=(0, 1)):
        for side in sides:
            form(i, p, side)
        at = pl.ds(pl.multiple_of(odd * half, half), half)
        for t in range(2):
            near[t, i, p, at] = (
                picked(mode_near.at[t], REACH, t)
                + picked(mode_near.at[t], REACH + 2 * t - 1, 1 - t)
            )
        near_half(i, p, 1 - odd, odd).start()

    def targets(side):
        return [j for j, (d, t) in enumerate(messages) if t == side]

    def send(i, p, side):
        for j in targets(side):
            over(i, p, j, odd).start()

    def drain(i, side):
        whole = message.at[i, side]
        remote(whole, whole, kz_send.at[i, side], kz_recv.at[i], "kz",
               far(0, side)).wait_send()

    def collect(i, p):
        value = near[odd, i, p]
        for d in range(len(steps)):
            value = value + arrived[d, i, p]
        return value

    def place(j):
        group = pieces // PARTS
        block, rest = j // group, lax.rem(j, group)
        p, r = rest // (group // 2), lax.rem(rest, group // 2)
        return p, pl.ds(pl.multiple_of(block * (n // PARTS) + r * rows, rows), rows)

    def link(i, j):
        p, at = place(j)
        return remote(out_ref.at[energy_of(i), p, at], before.at[i, p, at],
                      sp_send.at[i], sp_recv.at[i, j], "sp", sp + 1)

    def chain_step(i, j):
        p, at = place(j)
        e = energy_of(i)

        @pl.when(sp > 0)
        def _():
            link(i, j).wait_recv()
            out_ref[e, p, at] = outer[at] * before[i, p, at] + inverse[i, p, at]

        @pl.when(sp == 0)
        def _():
            out_ref[e, p, at] = inverse[i, p, at]

        @pl.when(sp < sp_count - 1)
        def _():
            link(i, j).start()

    early = jnp.clip(pieces - (sp - 1) * (ROW_BLOCKS - 1), 0, pieces)

    def chain_part(i, first, last):
        @pl.loop(first, last)
        def _(j):
            chain_step(i, j)

    def invert(i):
        whole = near.at[odd, i, :, pl.ds(pl.multiple_of((1 - odd) * half, half), half)]
        remote(whole, whole, near_send, near_recv.at[i], "kz", sibling).wait_recv()
        whole = arrived.at[:, i]
        remote(whole, whole, kz_send.at[i, 0], kz_recv.at[i], "kz", far(0, 0)).wait_recv()
        e = energy_of(i)
        guess = guess_ref[e]
        shift = onsite_ref[...] - energy_ref[e]
        diagonal = (lax.broadcasted_iota(jnp.int32, (n, n), 0)
                    == lax.broadcasted_iota(jnp.int32, (n, n), 1))
        r_re = jnp.where(diagonal, 1.0 - guess * shift, 0.0) - guess * collect(i, 0)
        r_im = -guess * collect(i, 1)

        def stack(re, im):
            return tuple(
                jnp.concatenate([a, b], axis=0) for a, b in zip(split(re), split(im))
            )

        def sides(re, im):
            return split(re), split(im), split(re + im)

        def finish(products):
            re, im, both = products
            return re - im, both - re - im

        r_sides = sides(r_re, r_im)
        s_re, s_im = finish([dot_split(side, side) for side in r_sides])
        s_sides = sides(s_re, s_im)
        one = jnp.where(diagonal, 1.0, 0.0)
        s_stack = stack(s_re, s_im)
        fourth = stack(*finish([dot_split(side, side) for side in s_sides]))
        q_re, q_im = one + r_re + s_re, r_im + s_im
        for first, last in CUTS:
            at = slice(first * n // PARTS, last * n // PARTS)
            size = (last - first) * n // PARTS
            rows_left = tuple(complex_pair(a[at], b[at]) for a, b in zip(*r_sides[:2]))
            cube = dot_split(rows_left, s_stack)
            p_re, p_im = q_re[at] + cube[:size], q_im[at] + cube[size:]
            rows_left = tuple(complex_pair(a, b) for a, b in zip(split(p_re), split(p_im)))
            result = dot_split(rows_left, fourth)
            inverse[i, 0, at] = guess * (p_re + result[:size])
            inverse[i, 1, at] = guess * (p_im + result[size:])
            pl.when(sp == 0)(
                lambda: chain_part(i, first * pieces // PARTS, last * pieces // PARTS)
            )

    if not direct:
        start_up()
        green_load.wait()
        for p in range(2):
            load_block(0, p)
    for load in small_loads:
        load.wait()
    coupling_load.wait()
    for m in range(modes):
        at = slice(m * half, (m + 1) * half)
        here = pl.ds(pl.multiple_of(odd * half, half), half)
        high, low = split(coupling_ref[m, here])
        left3[at] = jnp.concatenate([high, high, low], axis=1)
        high, low = split(coupling_ref[m].T * weight_ref[m])
        right3[m] = jnp.concatenate([high, low, high], axis=0)
    if direct:
        start_up()
        for p in range(2):
            first_load(p).wait()
    block_terms(0, 0)
    for side in range(2):
        for d, t in messages:
            if t == side:
                mode_to_origin(d, t, t).wait_recv()
        if side == 0:
            form(0, 0, 0)
            send(0, 0, 0)
    mode_to_sibling(1 - odd).wait_recv()
    block_messages(0, 0, (1,))
    block_terms(0, 1)
    block_messages(0, 1)
    send(0, 1, 0)
    across = jnp.broadcast_to(hopping_ref[...], (n, n))
    outer[...] = across * across.T

    @pl.when(sp < sp_count - 1)
    def _():
        pl.semaphore_wait(ready.at[1], 1)

    if direct:
        green_load.wait()
    if energy_count > 1:
        load_block(1, 0)
    drain(0, 0)
    for p in range(2):
        send(0, p, 1)

    for i in range(energy_count):
        last = i == energy_count - 1

        def second(i=i, between=lambda: None):
            load_block(i + 1, 1)

            def gate():
                drain(i, 1)
                send(i + 1, 0, 0)

            block_terms(i + 1, 1, between, gate)
            block_messages(i + 1, 1)
            send(i + 1, 1, 0)

        def turn(i=i):
            drain(i + 1, 0)
            for p in range(2):
                send(i + 1, p, 1)

        if last:
            invert(i)
            drain(i, 1)
            pl.when(sp > 0)(lambda i=i: chain_part(i, 0, pieces))
            continue
        if i > 0:
            load_block(i + 1, 0)
        block_terms(i + 1, 0)
        block_messages(i + 1, 0)
        pl.when(odd == 1)(second)
        invert(i)

        @pl.when(odd == 0)
        def _():
            taken = []

            def between():
                step = len(taken)
                taken.append(TAKEN[step] if step < len(TAKEN) else 0)
                first, end = sum(taken[:step]), sum(taken)
                if first < end:
                    pl.when(sp == 1)(lambda: chain_part(i, first, end))

            second(between=between)
            begun = jnp.where(sp == 1, sum(taken), 0)
            pl.when(sp > 0)(lambda: chain_part(i, begun, early))
            turn()
            pl.when(sp > 0)(lambda: chain_part(i, early, pieces))

        @pl.when(odd == 1)
        def _():
            turn()
            pl.when(sp > 0)(lambda: chain_part(i, 0, pieces))

    mode_to_sibling(odd).wait_send()
    for d, t in messages:
        mode_to_origin(d, t, odd).wait_send()
    @pl.when(en < en_count - 1)
    def _():
        remote(green_in.at[energy_count - 1], halo.at[0], halo_send.at[0], halo_recv.at[0, 0],
               "en", en + 1).wait_send()

    @pl.when(en > 0)
    def _():
        remote(green_in.at[0], halo.at[1], halo_send.at[1], halo_recv.at[1, 0],
               "en", en - 1).wait_send()

    whole = blocks.at[odd]
    remote(whole, whole, block_send, block_recv.at[0, 0], "kz", sibling).wait_send()
    whole = near.at[1 - odd, :, :, pl.ds(pl.multiple_of(odd * half, half), half)]
    remote(whole, whole, near_send, near_recv.at[0], "kz", sibling).wait_send()

    @pl.when(sp < sp_count - 1)
    def _():
        for i in range(energy_count):
            remote(out_ref.at[energy_of(i)], before.at[i], sp_send.at[i], sp_recv.at[i, 0],
                   "sp", sp + 1).wait_send()


def body(sizes, green, coupling, phonon_weight, mode_index, onsite, hopping, energies, guess_scale):
    energy_count, n = green.shape[1], green.shape[-1]
    modes = coupling.shape[1]
    blocks = (energy_count, 2, n, n)
    steps = 2 if sizes[0] > 2 * REACH else 1
    halves = (energy_count, 2, 2, steps, n // 2, n)
    pieces = 2 * ROW_BLOCKS
    hbm = pl.BlockSpec(memory_space=pltpu.HBM)
    vmem = pl.BlockSpec(memory_space=pltpu.VMEM)
    columns = mode_index.shape[1]
    dma = pltpu.SemaphoreType.DMA
    out = pl.pallas_call(
        functools.partial(kernel, sizes),
        out_shape=jax.ShapeDtypeStruct(blocks, jnp.float32),
        in_specs=[hbm] * 8,
        out_specs=vmem,
        scratch_shapes=[
            pltpu.SMEM((2, columns), jnp.int32),
            pltpu.SMEM((2 * steps, columns), jnp.int32),
            pltpu.SMEM(phonon_weight.shape, jnp.float32),
            pltpu.SMEM((energy_count,), jnp.float32),
            pltpu.SMEM((energy_count,), jnp.float32),
            pltpu.VMEM(blocks, jnp.float32),
            pltpu.VMEM(coupling.shape[1:], jnp.float32),
            pltpu.VMEM((1, n), jnp.float32),
            pltpu.VMEM((1, n), jnp.float32),
            pltpu.VMEM((2, 2, n, n), jnp.float32),
            pltpu.VMEM((modes * n // 2, 3 * n), jnp.bfloat16),
            pltpu.VMEM((modes, 3 * n, n), jnp.bfloat16),
            pltpu.VMEM((modes, n, n), jnp.float32),
            pltpu.VMEM((2,) + blocks, jnp.float32),
            pltpu.VMEM((2,) + blocks, jnp.float32),
            pltpu.VMEM(halves, jnp.float32),
            pltpu.VMEM((steps,) + blocks, jnp.float32),
            pltpu.VMEM(blocks, jnp.float32),
            pltpu.VMEM(blocks, jnp.float32),
            pltpu.VMEM((n, n), jnp.float32),
            pltpu.SemaphoreType.REGULAR((2,)),
            dma((6,)),
            dma,
            dma,
            dma((2,)),
            dma((2 * steps + 1,)),
            dma((2 * steps + 1,)),
            dma((2,)),
            dma((2, 2)),
            dma,
            dma((energy_count, 2)),
            dma,
            dma((energy_count,)),
            dma((energy_count, 2)),
            dma((energy_count,)),
            dma((energy_count,)),
            dma((energy_count, pieces)),
        ],
        compiler_params=pltpu.CompilerParams(
            collective_id=0, has_side_effects=True, vmem_limit_bytes=50 << 20
        ),
    )(
        *(
            pltpu.with_memory_space_constraint(value, pltpu.HBM)
            for value in (
                mode_index[0], phonon_weight, energies, guess_scale.reshape(energy_count),
                green.reshape(blocks), coupling[0], onsite, hopping,
            )
        )
    )
    return out.reshape(1, energy_count, 1, 2, n, n)


def solution(mesh):
    placed = (
        P("kz", "en", "sp", None, None, None),
        P("sp", None, None, None),
        P(),
        P("kz", None),
        P("sp", None),
        P("sp", None),
        P("en"),
        P("kz", "en", "sp"),
    )
    sizes = tuple(mesh.shape[axis] for axis in ("kz", "en", "sp"))
    return jax.shard_map(
        functools.partial(body, sizes),
        mesh=mesh,
        in_specs=placed,
        out_specs=P("kz", "en", "sp", None, None, None),
        check_vma=False,
    )
```

```python
import functools

import jax
import jax.numpy as jnp
from jax import lax
from jax.experimental import pallas as pl
from jax.experimental.pallas import tpu as pltpu
from jax.sharding import PartitionSpec as P

REACH = 2
ROW_BLOCKS = 8
PARTS = 4
CUTS = ((0, 1), (1, 4))
TAKEN = (2, 1, 1, 1, 0, 1)
MESH = pl.DeviceIdType.MESH


def split(value):
    high = value.astype(jnp.bfloat16)
    return high, (value - high.astype(jnp.float32)).astype(jnp.bfloat16)


def dot_split(first, second):
    left = jnp.concatenate([first[0], first[0], first[1]], axis=1)
    right = jnp.concatenate([second[0], second[1], second[0]], axis=0)
    return jnp.dot(left, right, preferred_element_type=jnp.float32)


def complex_pair(re, im):
    return jnp.concatenate(
        [jnp.concatenate([re, -im], axis=1), jnp.concatenate([im, re], axis=1)], axis=0
    )


def kernel(
    sizes,
    mode_in, weight_in, energy_in, guess_in, green_in, coupling_in, onsite_in, hopping_in,
    out_ref,
    mode_near, mode_far, weight_ref, energy_ref, guess_ref,
    green_ref, coupling_ref, onsite_ref, hopping_ref,
    halo, left3, right3, terms, blocks, near, message, arrived, inverse, before, outer,
    ready, small_sem, coupling_sem, green_sem, first_sem, mode_send, mode_recv, halo_send, halo_recv,
    block_send, block_recv, near_send, near_recv, kz_send, kz_recv, sp_send, sp_recv,
):
    kz_count, en_count, sp_count = sizes
    energy_count, _, n, _ = green_ref.shape
    modes = coupling_ref.shape[0]
    ring = kz_count > 2 * REACH
    steps = (REACH, -REACH) if ring else (REACH,)
    messages = [(d, t) for d in range(len(steps)) for t in range(2)]
    half = n // 2
    rows = n // ROW_BLOCKS
    pieces = 2 * ROW_BLOCKS
    k, en, sp = lax.axis_index("kz"), lax.axis_index("en"), lax.axis_index("sp")
    odd = lax.rem(k, 2)
    base = k - odd
    sibling = base + 1 - odd

    def far(d, t):
        return lax.rem(base + t + steps[d] + kz_count, kz_count)

    def origin(d, t):
        return lax.rem(base + t - steps[d] + kz_count, kz_count)

    direct = en_count == 2 and energy_count == 2

    def first_load(p):
        return pltpu.make_async_copy(green_in.at[1 - en, p], blocks.at[odd, 0, p],
                                     first_sem.at[p])

    green_load = pltpu.make_async_copy(green_in, green_ref, green_sem)
    coupling_load = pltpu.make_async_copy(coupling_in, coupling_ref, coupling_sem)
    small_loads = [
        pltpu.make_async_copy(source, target, small_sem.at[index])
        for index, (source, target) in enumerate((
            (mode_in, mode_near.at[odd]), (weight_in, weight_ref), (energy_in, energy_ref),
            (guess_in, guess_ref), (onsite_in, onsite_ref), (hopping_in, hopping_ref),
        ))
    ]
    barrier = pltpu.get_barrier_semaphore()

    def greet(axis, index):
        pl.semaphore_signal(barrier, inc=1, device_id={axis: index}, device_id_type=MESH)

    greet("kz", sibling)
    for d, t in messages:
        greet("kz", far(d, t))
    for axis, here, count in (("en", en, en_count), ("sp", sp, sp_count)):
        pl.when(here < count - 1)(lambda axis=axis, here=here: greet(axis, here + 1))
    coupling_load.start()
    if direct:
        for p in range(2):
            first_load(p).start()
    for load in small_loads:
        load.start()
    green_load.start()
    expected = 1 + len(messages)
    for here in (en, sp):
        expected = expected + (here > 0).astype(jnp.int32)
    pl.semaphore_wait(barrier, expected)
    for index, (axis, here) in enumerate((("en", en), ("sp", sp))):
        @pl.when(here > 0)
        def _():
            pl.semaphore_signal(ready.at[index], inc=1, device_id={axis: here - 1},
                                device_id_type=MESH)

    def remote(source, target, send, recv, axis, index):
        return pltpu.make_async_remote_copy(
            src_ref=source, dst_ref=target, send_sem=send, recv_sem=recv,
            device_id={axis: index}, device_id_type=MESH,
        )

    def halo_up(p):
        return remote(green_in.at[energy_count - 1, p], halo.at[0, p],
                      halo_send.at[0], halo_recv.at[0, p], "en", en + 1)

    def halo_down(p):
        return remote(green_in.at[0, p], halo.at[1, p],
                      halo_send.at[1], halo_recv.at[1, p], "en", en - 1)

    def mode_to_sibling(parity):
        return remote(mode_in, mode_near.at[parity], mode_send.at[2 * len(steps)],
                      mode_recv.at[len(messages)], "kz", sibling)

    def mode_to_origin(d, t, slot):
        return remote(mode_in, mode_far.at[2 * d + slot], mode_send.at[2 * d + t],
                      mode_recv.at[2 * d + slot], "kz", origin(d, t))

    def swap(i, p, parity):
        source = green_in.at[1 - en, p] if direct and i == 0 else blocks.at[parity, i, p]
        return remote(source, blocks.at[parity, i, p], block_send, block_recv.at[i, p],
                      "kz", sibling)

    for d, t in messages:
        mode_to_origin(d, t, odd).start()
    mode_to_sibling(odd).start()
    if direct:
        for p in range(2):
            swap(0, p, odd).start()
    for p in range(2):
        pl.when(en > 0)(lambda p=p: halo_down(p).start())

    def start_up():
        @pl.when(en < en_count - 1)
        def _():
            pl.semaphore_wait(ready.at[0], 1)
            for p in range(2):
                halo_up(p).start()


    def energy_of(i):
        return lax.rem(i + en, energy_count)

    def load_block(i, p):
        e = energy_of(i)
        below = green_ref[jnp.maximum(e - 1, 0), p]
        above = green_ref[jnp.minimum(e + 1, energy_count - 1), p]

        @pl.when((e > 0) & (e < energy_count - 1))
        def _():
            blocks[odd, i, p] = below + above

        @pl.when((e == 0) & (en > 0))
        def _():
            halo_up(p).wait_recv()
            blocks[odd, i, p] = halo[0, p] + above

        @pl.when((e == 0) & (en == 0))
        def _():
            blocks[odd, i, p] = above

        @pl.when((e > 0) & (e == energy_count - 1) & (en < en_count - 1))
        def _():
            halo_down(p).wait_recv()
            blocks[odd, i, p] = below + halo[1, p]

        @pl.when((e > 0) & (e == energy_count - 1) & (en == en_count - 1))
        def _():
            blocks[odd, i, p] = below

        swap(i, p, odd).start()

    def columns(d, t, source):
        if source == t:
            if not ring:
                return (2 * REACH, 0)
            return (2 * REACH,) if d == 0 else (0,)
        if not ring or t == d:
            return (2 * REACH - 1,) if t == 0 else (1,)
        return ()

    def picked(row, column, source):
        other = 1 - odd if source else odd
        return terms[row[column], pl.ds(pl.multiple_of(other * half, half), half)]

    def over(i, p, j, side):
        d, t = messages[j]
        return remote(message.at[i, t, p, d],
                      arrived.at[d, i, p, pl.ds(pl.multiple_of(side * half, half), half)],
                      kz_send.at[i, t], kz_recv.at[i], "kz", far(d, t))

    def near_half(i, p, parity, side):
        at = near.at[parity, i, p, pl.ds(pl.multiple_of(side * half, half), half)]
        return remote(at, at, near_send, near_recv.at[i], "kz", sibling)

    def block_terms(i, p, between=lambda: None, gate=None):
        def product(parity):
            return dot_split((left3[:, :n], left3[:, 2 * n:]), split(blocks[parity, i, p]))

        if gate is None:
            swap(i, p, 1 - odd).wait_recv()
            first = [product(odd), product(1 - odd)]
        else:
            first = [product(odd)]
            between()
            gate()
            between()
            swap(i, p, 1 - odd).wait_recv()
            first.append(product(1 - odd))
        between()
        for m in range(modes):
            at = slice(m * half, (m + 1) * half)
            high, low = split(jnp.concatenate([first[0][at], first[1][at]], axis=0))
            terms[m] = jnp.dot(
                jnp.concatenate([high, high, low], axis=1), right3[m],
                preferred_element_type=jnp.float32,
            )
            between()

    def form(i, p, side):
        for d, t in messages:
            if t == side:
                message[i, t, p, d] = sum(
                    picked(mode_far.at[2 * d + t], column, source)
                    for source in range(2) for column in columns(d, t, source)
                )

    def block_messages(i, p, sides=(0, 1)):
        for side in sides:
            form(i, p, side)
        at = pl.ds(pl.multiple_of(odd * half, half), half)
        for t in range(2):
            near[t, i, p, at] = (
                picked(mode_near.at[t], REACH, t)
                + picked(mode_near.at[t], REACH + 2 * t - 1, 1 - t)
            )
        near_half(i, p, 1 - odd, odd).start()

    def targets(side):
        return [j for j, (d, t) in enumerate(messages) if t == side]

    def send(i, p, side):
        for j in targets(side):
            over(i, p, j, odd).start()

    def drain(i, side):
        whole = message.at[i, side]
        remote(whole, whole, kz_send.at[i, side], kz_recv.at[i], "kz",
               far(0, side)).wait_send()

    def collect(i, p):
        value = near[odd, i, p]
        for d in range(len(steps)):
            value = value + arrived[d, i, p]
        return value

    def place(j):
        group = pieces // PARTS
        block, rest = j // group, lax.rem(j, group)
        p, r = rest // (group // 2), lax.rem(rest, group // 2)
        return p, pl.ds(pl.multiple_of(block * (n // PARTS) + r * rows, rows), rows)

    def link(i, j):
        p, at = place(j)
        return remote(out_ref.at[energy_of(i), p, at], before.at[i, p, at],
                      sp_send.at[i], sp_recv.at[i, j], "sp", sp + 1)

    def chain_step(i, j):
        p, at = place(j)
        e = energy_of(i)

        @pl.when(sp > 0)
        def _():
            link(i, j).wait_recv()
            out_ref[e, p, at] = outer[at] * before[i, p, at] + inverse[i, p, at]

        @pl.when(sp == 0)
        def _():
            out_ref[e, p, at] = inverse[i, p, at]

        @pl.when(sp < sp_count - 1)
        def _():
            link(i, j).start()

    early = jnp.clip(pieces - (sp - 1) * (ROW_BLOCKS - 1), 0, pieces)

    def chain_part(i, first, last):
        @pl.loop(first, last)
        def _(j):
            chain_step(i, j)

    def invert(i):
        whole = near.at[odd, i, :, pl.ds(pl.multiple_of((1 - odd) * half, half), half)]
        remote(whole, whole, near_send, near_recv.at[i], "kz", sibling).wait_recv()
        whole = arrived.at[:, i]
        remote(whole, whole, kz_send.at[i, 0], kz_recv.at[i], "kz", far(0, 0)).wait_recv()
        e = energy_of(i)
        guess = guess_ref[e]
        shift = onsite_ref[...] - energy_ref[e]
        diagonal = (lax.broadcasted_iota(jnp.int32, (n, n), 0)
                    == lax.broadcasted_iota(jnp.int32, (n, n), 1))
        r_re = jnp.where(diagonal, 1.0 - guess * shift, 0.0) - guess * collect(i, 0)
        r_im = -guess * collect(i, 1)

        def stack(re, im):
            return tuple(
                jnp.concatenate([a, b], axis=0) for a, b in zip(split(re), split(im))
            )

        def sides(re, im):
            return split(re), split(im), split(re + im)

        def finish(products):
            re, im, both = products
            return re - im, both - re - im

        r_sides = sides(r_re, r_im)
        s_re, s_im = finish([dot_split(side, side) for side in r_sides])
        s_sides = sides(s_re, s_im)
        one = jnp.where(diagonal, 1.0, 0.0)
        s_stack = stack(s_re, s_im)
        fourth = stack(*finish([dot_split(side, side) for side in s_sides]))
        q_re, q_im = one + r_re + s_re, r_im + s_im
        for first, last in CUTS:
            at = slice(first * n // PARTS, last * n // PARTS)
            size = (last - first) * n // PARTS
            rows_left = tuple(complex_pair(a[at], b[at]) for a, b in zip(*r_sides[:2]))
            cube = dot_split(rows_left, s_stack)
            p_re, p_im = q_re[at] + cube[:size], q_im[at] + cube[size:]
            rows_left = tuple(complex_pair(a, b) for a, b in zip(split(p_re), split(p_im)))
            result = dot_split(rows_left, fourth)
            inverse[i, 0, at] = guess * (p_re + result[:size])
            inverse[i, 1, at] = guess * (p_im + result[size:])
            pl.when(sp == 0)(
                lambda: chain_part(i, first * pieces // PARTS, last * pieces // PARTS)
            )

    if not direct:
        start_up()
        green_load.wait()
        for p in range(2):
            load_block(0, p)
    for load in small_loads:
        load.wait()
    coupling_load.wait()
    for m in range(modes):
        at = slice(m * half, (m + 1) * half)
        here = pl.ds(pl.multiple_of(odd * half, half), half)
        high, low = split(coupling_ref[m, here])
        left3[at] = jnp.concatenate([high, high, low], axis=1)
        high, low = split(coupling_ref[m].T * weight_ref[m])
        right3[m] = jnp.concatenate([high, low, high], axis=0)
    if direct:
        start_up()
        for p in range(2):
            first_load(p).wait()
    block_terms(0, 0)
    for side in range(2):
        for d, t in messages:
            if t == side:
                mode_to_origin(d, t, t).wait_recv()
        if side == 0:
            form(0, 0, 0)
            send(0, 0, 0)
    mode_to_sibling(1 - odd).wait_recv()
    block_messages(0, 0, (1,))
    block_terms(0, 1)
    block_messages(0, 1)
    send(0, 1, 0)
    across = jnp.broadcast_to(hopping_ref[...], (n, n))
    outer[...] = across * across.T

    @pl.when(sp < sp_count - 1)
    def _():
        pl.semaphore_wait(ready.at[1], 1)

    if direct:
        green_load.wait()
    if energy_count > 1:
        load_block(1, 0)
    drain(0, 0)
    for p in range(2):
        send(0, p, 1)

    for i in range(energy_count):
        last = i == energy_count - 1

        def second(i=i, between=lambda: None):
            load_block(i + 1, 1)

            def gate():
                drain(i, 1)
                send(i + 1, 0, 0)

            block_terms(i + 1, 1, between, gate)
            block_messages(i + 1, 1)
            send(i + 1, 1, 0)

        def turn(i=i):
            drain(i + 1, 0)
            for p in range(2):
                send(i + 1, p, 1)

        if last:
            invert(i)
            pl.when(sp > 0)(lambda i=i: chain_part(i, 0, pieces))
            drain(i, 1)
            continue
        if i > 0:
            load_block(i + 1, 0)
        block_terms(i + 1, 0)
        block_messages(i + 1, 0)
        pl.when(odd == 1)(second)
        invert(i)

        @pl.when(odd == 0)
        def _():
            taken = []

            def between():
                step = len(taken)
                taken.append(TAKEN[step] if step < len(TAKEN) else 0)
                first, end = sum(taken[:step]), sum(taken)
                if first < end:
                    pl.when(sp == 1)(lambda: chain_part(i, first, end))

            second(between=between)
            begun = jnp.where(sp == 1, sum(taken), 0)
            pl.when(sp > 0)(lambda: chain_part(i, begun, early))
            turn()
            pl.when(sp > 0)(lambda: chain_part(i, early, pieces))

        @pl.when(odd == 1)
        def _():
            turn()
            pl.when(sp > 0)(lambda: chain_part(i, 0, pieces))

    mode_to_sibling(odd).wait_send()
    for d, t in messages:
        mode_to_origin(d, t, odd).wait_send()
    @pl.when(en < en_count - 1)
    def _():
        remote(green_in.at[energy_count - 1], halo.at[0], halo_send.at[0], halo_recv.at[0, 0],
               "en", en + 1).wait_send()

    @pl.when(en > 0)
    def _():
        remote(green_in.at[0], halo.at[1], halo_send.at[1], halo_recv.at[1, 0],
               "en", en - 1).wait_send()

    whole = blocks.at[odd]
    remote(whole, whole, block_send, block_recv.at[0, 0], "kz", sibling).wait_send()
    whole = near.at[1 - odd, :, :, pl.ds(pl.multiple_of(odd * half, half), half)]
    remote(whole, whole, near_send, near_recv.at[0], "kz", sibling).wait_send()

    @pl.when(sp < sp_count - 1)
    def _():
        for i in range(energy_count):
            remote(out_ref.at[energy_of(i)], before.at[i], sp_send.at[i], sp_recv.at[i, 0],
                   "sp", sp + 1).wait_send()


def body(sizes, green, coupling, phonon_weight, mode_index, onsite, hopping, energies, guess_scale):
    energy_count, n = green.shape[1], green.shape[-1]
    modes = coupling.shape[1]
    blocks = (energy_count, 2, n, n)
    steps = 2 if sizes[0] > 2 * REACH else 1
    halves = (energy_count, 2, 2, steps, n // 2, n)
    pieces = 2 * ROW_BLOCKS
    hbm = pl.BlockSpec(memory_space=pltpu.HBM)
    vmem = pl.BlockSpec(memory_space=pltpu.VMEM)
    columns = mode_index.shape[1]
    dma = pltpu.SemaphoreType.DMA
    out = pl.pallas_call(
        functools.partial(kernel, sizes),
        out_shape=jax.ShapeDtypeStruct(blocks, jnp.float32),
        in_specs=[hbm] * 8,
        out_specs=vmem,
        scratch_shapes=[
            pltpu.SMEM((2, columns), jnp.int32),
            pltpu.SMEM((2 * steps, columns), jnp.int32),
            pltpu.SMEM(phonon_weight.shape, jnp.float32),
            pltpu.SMEM((energy_count,), jnp.float32),
            pltpu.SMEM((energy_count,), jnp.float32),
            pltpu.VMEM(blocks, jnp.float32),
            pltpu.VMEM(coupling.shape[1:], jnp.float32),
            pltpu.VMEM((1, n), jnp.float32),
            pltpu.VMEM((1, n), jnp.float32),
            pltpu.VMEM((2, 2, n, n), jnp.float32),
            pltpu.VMEM((modes * n // 2, 3 * n), jnp.bfloat16),
            pltpu.VMEM((modes, 3 * n, n), jnp.bfloat16),
            pltpu.VMEM((modes, n, n), jnp.float32),
            pltpu.VMEM((2,) + blocks, jnp.float32),
            pltpu.VMEM((2,) + blocks, jnp.float32),
            pltpu.VMEM(halves, jnp.float32),
            pltpu.VMEM((steps,) + blocks, jnp.float32),
            pltpu.VMEM(blocks, jnp.float32),
            pltpu.VMEM(blocks, jnp.float32),
            pltpu.VMEM((n, n), jnp.float32),
            pltpu.SemaphoreType.REGULAR((2,)),
            dma((6,)),
            dma,
            dma,
            dma((2,)),
            dma((2 * steps + 1,)),
            dma((2 * steps + 1,)),
            dma((2,)),
            dma((2, 2)),
            dma,
            dma((energy_count, 2)),
            dma,
            dma((energy_count,)),
            dma((energy_count, 2)),
            dma((energy_count,)),
            dma((energy_count,)),
            dma((energy_count, pieces)),
        ],
        compiler_params=pltpu.CompilerParams(
            collective_id=0, has_side_effects=True, vmem_limit_bytes=50 << 20
        ),
    )(
        *(
            pltpu.with_memory_space_constraint(value, pltpu.HBM)
            for value in (
                mode_index[0], phonon_weight, energies, guess_scale.reshape(energy_count),
                green.reshape(blocks), coupling[0], onsite, hopping,
            )
        )
    )
    return out.reshape(1, energy_count, 1, 2, n, n)


def solution(mesh):
    placed = (
        P("kz", "en", "sp", None, None, None),
        P("sp", None, None, None),
        P(),
        P("kz", None),
        P("sp", None),
        P("sp", None),
        P("en"),
        P("kz", "en", "sp"),
    )
    sizes = tuple(mesh.shape[axis] for axis in ("kz", "en", "sp"))
    return jax.shard_map(
        functools.partial(body, sizes),
        mesh=mesh,
        in_specs=placed,
        out_specs=P("kz", "en", "sp", None, None, None),
        check_vma=False,
    )
```

```python
import functools

import jax
import jax.numpy as jnp
from jax import lax
from jax.experimental import pallas as pl
from jax.experimental.pallas import tpu as pltpu
from jax.sharding import PartitionSpec as P

REACH = 2
ROW_BLOCKS = 8
PARTS = 4
CUTS = ((0, 1), (1, 4))
TAKEN = (1, 1, 2, 1, 0, 1)
MESH = pl.DeviceIdType.MESH


def split(value):
    high = value.astype(jnp.bfloat16)
    return high, (value - high.astype(jnp.float32)).astype(jnp.bfloat16)


def dot_split(first, second):
    left = jnp.concatenate([first[0], first[0], first[1]], axis=1)
    right = jnp.concatenate([second[0], second[1], second[0]], axis=0)
    return jnp.dot(left, right, preferred_element_type=jnp.float32)


def complex_pair(re, im):
    return jnp.concatenate(
        [jnp.concatenate([re, -im], axis=1), jnp.concatenate([im, re], axis=1)], axis=0
    )


def kernel(
    sizes,
    mode_in, weight_in, energy_in, guess_in, green_in, coupling_in, onsite_in, hopping_in,
    out_ref,
    mode_near, mode_far, weight_ref, energy_ref, guess_ref,
    green_ref, coupling_ref, onsite_ref, hopping_ref,
    halo, left3, right3, terms, blocks, near, message, arrived, inverse, before, outer,
    ready, small_sem, coupling_sem, green_sem, first_sem, mode_send, mode_recv, halo_send, halo_recv,
    block_send, block_recv, near_send, near_recv, kz_send, kz_recv, sp_send, sp_recv,
):
    kz_count, en_count, sp_count = sizes
    energy_count, _, n, _ = green_ref.shape
    modes = coupling_ref.shape[0]
    ring = kz_count > 2 * REACH
    steps = (REACH, -REACH) if ring else (REACH,)
    messages = [(d, t) for d in range(len(steps)) for t in range(2)]
    half = n // 2
    rows = n // ROW_BLOCKS
    pieces = 2 * ROW_BLOCKS
    k, en, sp = lax.axis_index("kz"), lax.axis_index("en"), lax.axis_index("sp")
    odd = lax.rem(k, 2)
    base = k - odd
    sibling = base + 1 - odd

    def far(d, t):
        return lax.rem(base + t + steps[d] + kz_count, kz_count)

    def origin(d, t):
        return lax.rem(base + t - steps[d] + kz_count, kz_count)

    direct = en_count == 2 and energy_count == 2

    def first_load():
        return pltpu.make_async_copy(green_in.at[1 - en], blocks.at[odd, 0], first_sem)

    green_load = pltpu.make_async_copy(green_in, green_ref, green_sem)
    coupling_load = pltpu.make_async_copy(coupling_in, coupling_ref, coupling_sem)
    small_loads = [
        pltpu.make_async_copy(source, target, small_sem.at[index])
        for index, (source, target) in enumerate((
            (mode_in, mode_near.at[odd]), (weight_in, weight_ref), (energy_in, energy_ref),
            (guess_in, guess_ref), (onsite_in, onsite_ref), (hopping_in, hopping_ref),
        ))
    ]
    barrier = pltpu.get_barrier_semaphore()

    def greet(axis, index):
        pl.semaphore_signal(barrier, inc=1, device_id={axis: index}, device_id_type=MESH)

    greet("kz", sibling)
    for d, t in messages:
        greet("kz", far(d, t))
    for axis, here, count in (("en", en, en_count), ("sp", sp, sp_count)):
        pl.when(here < count - 1)(lambda axis=axis, here=here: greet(axis, here + 1))
    coupling_load.start()
    if direct:
        first_load().start()
    for load in small_loads:
        load.start()
    green_load.start()
    expected = 1 + len(messages)
    for here in (en, sp):
        expected = expected + (here > 0).astype(jnp.int32)
    pl.semaphore_wait(barrier, expected)
    for index, (axis, here) in enumerate((("en", en), ("sp", sp))):
        @pl.when(here > 0)
        def _():
            pl.semaphore_signal(ready.at[index], inc=1, device_id={axis: here - 1},
                                device_id_type=MESH)

    def remote(source, target, send, recv, axis, index):
        return pltpu.make_async_remote_copy(
            src_ref=source, dst_ref=target, send_sem=send, recv_sem=recv,
            device_id={axis: index}, device_id_type=MESH,
        )

    def halo_up(p):
        return remote(green_in.at[energy_count - 1, p], halo.at[0, p],
                      halo_send.at[0], halo_recv.at[0, p], "en", en + 1)

    def halo_down(p):
        return remote(green_in.at[0, p], halo.at[1, p],
                      halo_send.at[1], halo_recv.at[1, p], "en", en - 1)

    def mode_to_sibling(parity):
        return remote(mode_in, mode_near.at[parity], mode_send.at[2 * len(steps)],
                      mode_recv.at[len(messages)], "kz", sibling)

    def mode_to_origin(d, t, slot):
        return remote(mode_in, mode_far.at[2 * d + slot], mode_send.at[2 * d + t],
                      mode_recv.at[2 * d + slot], "kz", origin(d, t))

    def swap(i, p, parity):
        source = green_in.at[1 - en, p] if direct and i == 0 else blocks.at[parity, i, p]
        return remote(source, blocks.at[parity, i, p], block_send, block_recv.at[i, p],
                      "kz", sibling)

    for d, t in messages:
        mode_to_origin(d, t, odd).start()
    mode_to_sibling(odd).start()
    if direct:
        for p in range(2):
            swap(0, p, odd).start()
    for p in range(2):
        pl.when(en > 0)(lambda p=p: halo_down(p).start())

    def start_up():
        @pl.when(en < en_count - 1)
        def _():
            pl.semaphore_wait(ready.at[0], 1)
            for p in range(2):
                halo_up(p).start()


    def energy_of(i):
        return lax.rem(i + en, energy_count)

    def load_block(i, p):
        e = energy_of(i)
        below = green_ref[jnp.maximum(e - 1, 0), p]
        above = green_ref[jnp.minimum(e + 1, energy_count - 1), p]

        @pl.when((e > 0) & (e < energy_count - 1))
        def _():
            blocks[odd, i, p] = below + above

        @pl.when((e == 0) & (en > 0))
        def _():
            halo_up(p).wait_recv()
            blocks[odd, i, p] = halo[0, p] + above

        @pl.when((e == 0) & (en == 0))
        def _():
            blocks[odd, i, p] = above

        @pl.when((e > 0) & (e == energy_count - 1) & (en < en_count - 1))
        def _():
            halo_down(p).wait_recv()
            blocks[odd, i, p] = below + halo[1, p]

        @pl.when((e > 0) & (e == energy_count - 1) & (en == en_count - 1))
        def _():
            blocks[odd, i, p] = below

        swap(i, p, odd).start()

    def columns(d, t, source):
        if source == t:
            if not ring:
                return (2 * REACH, 0)
            return (2 * REACH,) if d == 0 else (0,)
        if not ring or t == d:
            return (2 * REACH - 1,) if t == 0 else (1,)
        return ()

    def picked(row, column, source):
        other = 1 - odd if source else odd
        return terms[row[column], pl.ds(pl.multiple_of(other * half, half), half)]

    def over(i, p, j, side):
        d, t = messages[j]
        return remote(message.at[i, t, p, d],
                      arrived.at[d, i, p, pl.ds(pl.multiple_of(side * half, half), half)],
                      kz_send.at[i, t], kz_recv.at[i], "kz", far(d, t))

    def near_half(i, p, parity, side):
        at = near.at[parity, i, p, pl.ds(pl.multiple_of(side * half, half), half)]
        return remote(at, at, near_send, near_recv.at[i], "kz", sibling)

    def block_terms(i, p, between=lambda: None, gate=None):
        def product(parity):
            return dot_split((left3[:, :n], left3[:, 2 * n:]), split(blocks[parity, i, p]))

        if gate is None:
            swap(i, p, 1 - odd).wait_recv()
            first = [product(odd), product(1 - odd)]
        else:
            first = [product(odd)]
            between()
            gate()
            between()
            swap(i, p, 1 - odd).wait_recv()
            first.append(product(1 - odd))
        between()
        for m in range(modes):
            at = slice(m * half, (m + 1) * half)
            high, low = split(jnp.concatenate([first[0][at], first[1][at]], axis=0))
            terms[m] = jnp.dot(
                jnp.concatenate([high, high, low], axis=1), right3[m],
                preferred_element_type=jnp.float32,
            )
            between()

    def form(i, p, side):
        for d, t in messages:
            if t == side:
                message[i, t, p, d] = sum(
                    picked(mode_far.at[2 * d + t], column, source)
                    for source in range(2) for column in columns(d, t, source)
                )

    def block_messages(i, p, sides=(0, 1)):
        for side in sides:
            form(i, p, side)
        at = pl.ds(pl.multiple_of(odd * half, half), half)
        for t in range(2):
            near[t, i, p, at] = (
                picked(mode_near.at[t], REACH, t)
                + picked(mode_near.at[t], REACH + 2 * t - 1, 1 - t)
            )
        near_half(i, p, 1 - odd, odd).start()

    def targets(side):
        return [j for j, (d, t) in enumerate(messages) if t == side]

    def send(i, p, side):
        for j in targets(side):
            over(i, p, j, odd).start()

    def drain(i, side):
        whole = message.at[i, side]
        remote(whole, whole, kz_send.at[i, side], kz_recv.at[i], "kz",
               far(0, side)).wait_send()

    def collect(i, p):
        value = near[odd, i, p]
        for d in range(len(steps)):
            value = value + arrived[d, i, p]
        return value

    def place(j):
        group = pieces // PARTS
        block, rest = j // group, lax.rem(j, group)
        p, r = rest // (group // 2), lax.rem(rest, group // 2)
        return p, pl.ds(pl.multiple_of(block * (n // PARTS) + r * rows, rows), rows)

    def link(i, j):
        p, at = place(j)
        return remote(out_ref.at[energy_of(i), p, at], before.at[i, p, at],
                      sp_send.at[i], sp_recv.at[i, j], "sp", sp + 1)

    def chain_step(i, j):
        p, at = place(j)
        e = energy_of(i)

        @pl.when(sp > 0)
        def _():
            link(i, j).wait_recv()
            out_ref[e, p, at] = outer[at] * before[i, p, at] + inverse[i, p, at]

        @pl.when(sp == 0)
        def _():
            out_ref[e, p, at] = inverse[i, p, at]

        @pl.when(sp < sp_count - 1)
        def _():
            link(i, j).start()

    early = jnp.clip(pieces - (sp - 1) * (ROW_BLOCKS - 1), 0, pieces)

    def chain_part(i, first, last):
        @pl.loop(first, last)
        def _(j):
            chain_step(i, j)

    def invert(i):
        whole = near.at[odd, i, :, pl.ds(pl.multiple_of((1 - odd) * half, half), half)]
        remote(whole, whole, near_send, near_recv.at[i], "kz", sibling).wait_recv()
        whole = arrived.at[:, i]
        remote(whole, whole, kz_send.at[i, 0], kz_recv.at[i], "kz", far(0, 0)).wait_recv()
        e = energy_of(i)
        guess = guess_ref[e]
        shift = onsite_ref[...] - energy_ref[e]
        diagonal = (lax.broadcasted_iota(jnp.int32, (n, n), 0)
                    == lax.broadcasted_iota(jnp.int32, (n, n), 1))
        r_re = jnp.where(diagonal, 1.0 - guess * shift, 0.0) - guess * collect(i, 0)
        r_im = -guess * collect(i, 1)

        def stack(re, im):
            return tuple(
                jnp.concatenate([a, b], axis=0) for a, b in zip(split(re), split(im))
            )

        def sides(re, im):
            return split(re), split(im), split(re + im)

        def finish(products):
            re, im, both = products
            return re - im, both - re - im

        r_sides = sides(r_re, r_im)
        s_re, s_im = finish([dot_split(side, side) for side in r_sides])
        s_sides = sides(s_re, s_im)
        one = jnp.where(diagonal, 1.0, 0.0)
        s_stack = stack(s_re, s_im)
        fourth = stack(*finish([dot_split(side, side) for side in s_sides]))
        q_re, q_im = one + r_re + s_re, r_im + s_im
        for first, last in CUTS:
            at = slice(first * n // PARTS, last * n // PARTS)
            size = (last - first) * n // PARTS
            rows_left = tuple(complex_pair(a[at], b[at]) for a, b in zip(*r_sides[:2]))
            cube = dot_split(rows_left, s_stack)
            p_re, p_im = q_re[at] + cube[:size], q_im[at] + cube[size:]
            rows_left = tuple(complex_pair(a, b) for a, b in zip(split(p_re), split(p_im)))
            result = dot_split(rows_left, fourth)
            inverse[i, 0, at] = guess * (p_re + result[:size])
            inverse[i, 1, at] = guess * (p_im + result[size:])
            pl.when(sp == 0)(
                lambda: chain_part(i, first * pieces // PARTS, last * pieces // PARTS)
            )

    if not direct:
        start_up()
        green_load.wait()
        for p in range(2):
            load_block(0, p)
    for load in small_loads:
        load.wait()
    coupling_load.wait()
    for m in range(modes):
        at = slice(m * half, (m + 1) * half)
        here = pl.ds(pl.multiple_of(odd * half, half), half)
        high, low = split(coupling_ref[m, here])
        left3[at] = jnp.concatenate([high, high, low], axis=1)
        high, low = split(coupling_ref[m].T * weight_ref[m])
        right3[m] = jnp.concatenate([high, low, high], axis=0)
    if direct:
        start_up()
        first_load().wait()
    block_terms(0, 0)
    for side in range(2):
        for d, t in messages:
            if t == side:
                mode_to_origin(d, t, t).wait_recv()
        if side == 0:
            form(0, 0, 0)
            send(0, 0, 0)
    mode_to_sibling(1 - odd).wait_recv()
    block_messages(0, 0, (1,))
    block_terms(0, 1)
    block_messages(0, 1)
    send(0, 1, 0)
    across = jnp.broadcast_to(hopping_ref[...], (n, n))
    outer[...] = across * across.T

    @pl.when(sp < sp_count - 1)
    def _():
        pl.semaphore_wait(ready.at[1], 1)

    if direct:
        green_load.wait()
    if energy_count > 1:
        load_block(1, 0)
    drain(0, 0)
    for p in range(2):
        send(0, p, 1)

    for i in range(energy_count):
        last = i == energy_count - 1

        def second(i=i, between=lambda: None):
            load_block(i + 1, 1)

            def gate():
                drain(i, 1)
                send(i + 1, 0, 0)

            block_terms(i + 1, 1, between, gate)
            block_messages(i + 1, 1)
            send(i + 1, 1, 0)

        def turn(i=i):
            drain(i + 1, 0)
            for p in range(2):
                send(i + 1, p, 1)

        if last:
            invert(i)
            pl.when(sp > 0)(lambda i=i: chain_part(i, 0, pieces))
            drain(i, 1)
            continue
        if i > 0:
            load_block(i + 1, 0)
        block_terms(i + 1, 0)
        block_messages(i + 1, 0)
        pl.when(odd == 1)(second)
        invert(i)

        @pl.when(odd == 0)
        def _():
            taken = []

            def between():
                step = len(taken)
                taken.append(TAKEN[step] if step < len(TAKEN) else 0)
                first, end = sum(taken[:step]), sum(taken)
                if first < end:
                    pl.when(sp == 1)(lambda: chain_part(i, first, end))

            second(between=between)
            begun = jnp.where(sp == 1, sum(taken), 0)
            pl.when(sp > 0)(lambda: chain_part(i, begun, early))
            turn()
            pl.when(sp > 0)(lambda: chain_part(i, early, pieces))

        @pl.when(odd == 1)
        def _():
            turn()
            pl.when(sp > 0)(lambda: chain_part(i, 0, pieces))

    mode_to_sibling(odd).wait_send()
    for d, t in messages:
        mode_to_origin(d, t, odd).wait_send()
    @pl.when(en < en_count - 1)
    def _():
        remote(green_in.at[energy_count - 1], halo.at[0], halo_send.at[0], halo_recv.at[0, 0],
               "en", en + 1).wait_send()

    @pl.when(en > 0)
    def _():
        remote(green_in.at[0], halo.at[1], halo_send.at[1], halo_recv.at[1, 0],
               "en", en - 1).wait_send()

    whole = blocks.at[odd]
    remote(whole, whole, block_send, block_recv.at[0, 0], "kz", sibling).wait_send()
    whole = near.at[1 - odd, :, :, pl.ds(pl.multiple_of(odd * half, half), half)]
    remote(whole, whole, near_send, near_recv.at[0], "kz", sibling).wait_send()

    @pl.when(sp < sp_count - 1)
    def _():
        for i in range(energy_count):
            remote(out_ref.at[energy_of(i)], before.at[i], sp_send.at[i], sp_recv.at[i, 0],
                   "sp", sp + 1).wait_send()


def body(sizes, green, coupling, phonon_weight, mode_index, onsite, hopping, energies, guess_scale):
    energy_count, n = green.shape[1], green.shape[-1]
    modes = coupling.shape[1]
    blocks = (energy_count, 2, n, n)
    steps = 2 if sizes[0] > 2 * REACH else 1
    halves = (energy_count, 2, 2, steps, n // 2, n)
    pieces = 2 * ROW_BLOCKS
    hbm = pl.BlockSpec(memory_space=pltpu.HBM)
    vmem = pl.BlockSpec(memory_space=pltpu.VMEM)
    columns = mode_index.shape[1]
    dma = pltpu.SemaphoreType.DMA
    out = pl.pallas_call(
        functools.partial(kernel, sizes),
        out_shape=jax.ShapeDtypeStruct(blocks, jnp.float32),
        in_specs=[hbm] * 8,
        out_specs=vmem,
        scratch_shapes=[
            pltpu.SMEM((2, columns), jnp.int32),
            pltpu.SMEM((2 * steps, columns), jnp.int32),
            pltpu.SMEM(phonon_weight.shape, jnp.float32),
            pltpu.SMEM((energy_count,), jnp.float32),
            pltpu.SMEM((energy_count,), jnp.float32),
            pltpu.VMEM(blocks, jnp.float32),
            pltpu.VMEM(coupling.shape[1:], jnp.float32),
            pltpu.VMEM((1, n), jnp.float32),
            pltpu.VMEM((1, n), jnp.float32),
            pltpu.VMEM((2, 2, n, n), jnp.float32),
            pltpu.VMEM((modes * n // 2, 3 * n), jnp.bfloat16),
            pltpu.VMEM((modes, 3 * n, n), jnp.bfloat16),
            pltpu.VMEM((modes, n, n), jnp.float32),
            pltpu.VMEM((2,) + blocks, jnp.float32),
            pltpu.VMEM((2,) + blocks, jnp.float32),
            pltpu.VMEM(halves, jnp.float32),
            pltpu.VMEM((steps,) + blocks, jnp.float32),
            pltpu.VMEM(blocks, jnp.float32),
            pltpu.VMEM(blocks, jnp.float32),
            pltpu.VMEM((n, n), jnp.float32),
            pltpu.SemaphoreType.REGULAR((2,)),
            dma((6,)),
            dma,
            dma,
            dma,
            dma((2 * steps + 1,)),
            dma((2 * steps + 1,)),
            dma((2,)),
            dma((2, 2)),
            dma,
            dma((energy_count, 2)),
            dma,
            dma((energy_count,)),
            dma((energy_count, 2)),
            dma((energy_count,)),
            dma((energy_count,)),
            dma((energy_count, pieces)),
        ],
        compiler_params=pltpu.CompilerParams(
            collective_id=0, has_side_effects=True, vmem_limit_bytes=50 << 20
        ),
    )(
        *(
            pltpu.with_memory_space_constraint(value, pltpu.HBM)
            for value in (
                mode_index[0], phonon_weight, energies, guess_scale.reshape(energy_count),
                green.reshape(blocks), coupling[0], onsite, hopping,
            )
        )
    )
    return out.reshape(1, energy_count, 1, 2, n, n)


def solution(mesh):
    placed = (
        P("kz", "en", "sp", None, None, None),
        P("sp", None, None, None),
        P(),
        P("kz", None),
        P("sp", None),
        P("sp", None),
        P("en"),
        P("kz", "en", "sp"),
    )
    sizes = tuple(mesh.shape[axis] for axis in ("kz", "en", "sp"))
    return jax.shard_map(
        functools.partial(body, sizes),
        mesh=mesh,
        in_specs=placed,
        out_specs=P("kz", "en", "sp", None, None, None),
        check_vma=False,
    )
```
